32 devices in a mesh: shard: 4 (over z), ctx: 4 (over y, core), tp: 2 (over x).
Axes of the slice: x: 2, y: 2, z: 4, core: 2. Of those that a mesh axis runs over, the one named last changes fastest.
Arguments:
- block_input: float32 [2048, 640], P(('shard', 'ctx')), may hold values from -6 to 6
- out_cotangent: float32 [2048, 640], P(('shard', 'ctx')), may hold values from -6 to 6
- seq_lengths: int32 [4, 4], P('shard'), may hold values from 1 to 256, 512 in all within a row
- q_weight: bfloat16 [640, 1024], P('shard', 'tp'), may hold values from -0.25 to 0.25
- k_weight: bfloat16 [640, 256], P('shard'), may hold values from -0.25 to 0.25
- v_weight: bfloat16 [640, 256], P('shard'), may hold values from -0.25 to 0.25
- o_weight: bfloat16 [640, 1024], P('shard', 'tp'), may hold values from -0.1875 to 0.1875
- gate_weight: bfloat16 [640, 2048], P('shard', 'tp'), may hold values from -0.25 to 0.25
- up_weight: bfloat16 [640, 2048], P('shard', 'tp'), may hold values from -0.25 to 0.25
- down_weight: bfloat16 [640, 2048], P('shard', 'tp'), may hold values from -0.125 to 0.125
- attn_in_gain: bfloat16 [640], P('shard'), may hold values from 0.25 to 1.75
- attn_out_gain: bfloat16 [640], P('shard'), may hold values from 0.25 to 1.75
- ffn_in_gain: bfloat16 [640], P('shard'), may hold values from 0.25 to 1.75
- ffn_out_gain: bfloat16 [640], P('shard'), may hold values from 0.25 to 1.75
- query_gain: bfloat16 [256], P('shard'), may hold values from 0.25 to 1.75
- key_gain: bfloat16 [256], P('shard'), may hold values from 0.25 to 1.75
Outputs:
- block_output: float32 [2048, 640], P(('shard', 'ctx'))
- input_grad: float32 [2048, 640], P(('shard', 'ctx'))
- q_weight_grad: float32 [640, 1024], P('shard', 'tp')
- k_weight_grad: float32 [640, 256], P('shard')
- v_weight_grad: float32 [640, 256], P('shard')
- o_weight_grad: float32 [640, 1024], P('shard', 'tp')
- gate_weight_grad: float32 [640, 2048], P('shard', 'tp')
- up_weight_grad: float32 [640, 2048], P('shard', 'tp')
- down_weight_grad: float32 [640, 2048], P('shard', 'tp')
- attn_in_gain_grad: float32 [640], P('shard')
- attn_out_gain_grad: float32 [640], P('shard')
- ffn_in_gain_grad: float32 [640], P('shard')
- ffn_out_gain_grad: float32 [640], P('shard')
- query_gain_grad: float32 [256], P('shard')
- key_gain_grad: float32 [256], P('shard')
The draws below stay inside these ranges and needn't reach their ends.
Inputs may be any that keep to these rules, and one draw needn't show every extreme that they name: Row b of seq_lengths lists the 4 sequences packed into row b in order; they sum to 512, and the longest of every row has exactly 256 tokens.
All inputs are finite; a program needn't handle non-finite values.
Results may differ from the reference program's by a relative error of at most 0.015.
Values may be sent and summed in bfloat16 or wider, within the bound.
A program may use at most 64 MiB of HBM per device.

```python
import math
import jax
import jax.numpy as jnp
import numpy as np
from jax import lax

D = 640
HEADS = 4
HD = 256
FF = 2048
SEQS = 4
LENGTH = 512
MOST = 256
TOKENS = 2048
N_SHARD = 4


def levels(rng, extent, split, low, high):
    gain, own = 1.0, jax.random.fold_in(rng, 6)
    for axis_at, blocks in split:
        steps = jnp.exp(jax.random.uniform(jax.random.fold_in(own, axis_at), (blocks,), jnp.float32, low / len(split), high / len(split)))
        gain = gain * jnp.repeat(steps, extent[axis_at] // blocks).reshape([-1 if axis == axis_at else 1 for axis in range(len(extent))])
    return gain


def length_profile(count, total, limit, skew):
    loads = [(1 << 20) // math.isqrt(standing ** skew) + 1 for standing in range(2, count + 1)]
    surplus, given = total - limit - (count - 1), [1] * (count - 1)
    while surplus > 0:
        movable = [i for i in range(count - 1) if given[i] < limit]
        pool, left = sum([loads[i] for i in movable]), surplus
        for i in movable:
            extra = min(limit - given[i], max(1, left * loads[i] // pool), surplus)
            given[i] = given[i] + extra
            surplus = surplus - extra
    return np.array([limit] + given)


def ragged(rng, count, total, most, skew):
    if count == 2:
        one = jax.random.randint(rng, (), max(1, total - most), min(most, total - 1) + 1)
        return jnp.stack([one, total - one])
    sizes = jnp.asarray(length_profile(count, total, most, skew), jnp.int32)
    twos = (count - 1) // 2
    giver, taker = sizes[1:1 + 2 * twos:2], sizes[2:2 + 2 * twos:2]
    room = jnp.minimum(giver - 1, most - taker)
    moved = jax.random.randint(jax.random.fold_in(rng, 1), (twos,), 0, 1 << 20) % (room + 1)
    sizes = sizes.at[1:1 + 2 * twos:2].set(giver - moved).at[2:2 + 2 * twos:2].set(taker + moved)
    return sizes[jax.random.permutation(jax.random.fold_in(rng, 2), count)]


def gaussian(key, shape, deviation, reach, split=(), dtype=jnp.bfloat16):
    values = deviation * jax.random.normal(key, shape, jnp.float32)
    if split:
        values = values * levels(key, shape, split, -0.22, 0.18)
    return jnp.clip(values, -reach, reach).astype(dtype)


def setup_inputs(seed: int = 0) -> dict:
    arg_keys = jax.random.split(jax.random.key(seed), 17)
    block_input = gaussian(arg_keys[0], (TOKENS, D), 1.0, 6.0, ((0, 16),), jnp.float32)
    out_cotangent = gaussian(arg_keys[1], (TOKENS, D), 1.0, 6.0, ((0, 16),), jnp.float32)
    seq_lengths = jax.vmap(lambda own: ragged(own, SEQS, LENGTH, MOST, 2))(jax.random.split(arg_keys[2], N_SHARD)).reshape((N_SHARD, SEQS)).astype(jnp.int32)
    q_weight = gaussian(arg_keys[3], (D, HEADS * HD), D ** -0.5, 0.25, ((0, 4), (1, 2)))
    k_weight = gaussian(arg_keys[4], (D, HD), D ** -0.5, 0.25, ((0, 4),))
    v_weight = gaussian(arg_keys[5], (D, HD), D ** -0.5, 0.25, ((0, 4),))
    o_weight = gaussian(arg_keys[6], (D, HEADS * HD), (HEADS * HD) ** -0.5, 0.1875, ((0, 4), (1, 2)))
    gate_weight = gaussian(arg_keys[7], (D, FF), D ** -0.5, 0.25, ((0, 4), (1, 2)))
    up_weight = gaussian(arg_keys[8], (D, FF), D ** -0.5, 0.25, ((0, 4), (1, 2)))
    down_weight = gaussian(arg_keys[9], (D, FF), FF ** -0.5, 0.125, ((0, 4), (1, 2)))
    attn_in_gain = jnp.clip(1.0 + 0.15 * jax.random.normal(arg_keys[10], (D,), jnp.float32), 0.25, 1.75).astype(jnp.bfloat16)
    attn_out_gain = jnp.clip(1.0 + 0.15 * jax.random.normal(arg_keys[11], (D,), jnp.float32), 0.25, 1.75).astype(jnp.bfloat16)
    ffn_in_gain = jnp.clip(1.0 + 0.15 * jax.random.normal(arg_keys[12], (D,), jnp.float32), 0.25, 1.75).astype(jnp.bfloat16)
    ffn_out_gain = jnp.clip(1.0 + 0.15 * jax.random.normal(arg_keys[13], (D,), jnp.float32), 0.25, 1.75).astype(jnp.bfloat16)
    query_gain = jnp.clip(1.0 + 0.15 * jax.random.normal(arg_keys[14], (HD,), jnp.float32), 0.25, 1.75).astype(jnp.bfloat16)
    key_gain = jnp.clip(1.0 + 0.15 * jax.random.normal(arg_keys[15], (HD,), jnp.float32), 0.25, 1.75).astype(jnp.bfloat16)
    return dict(block_input=block_input, out_cotangent=out_cotangent, seq_lengths=seq_lengths, q_weight=q_weight, k_weight=k_weight, v_weight=v_weight, o_weight=o_weight, gate_weight=gate_weight, up_weight=up_weight, down_weight=down_weight, attn_in_gain=attn_in_gain, attn_out_gain=attn_out_gain, ffn_in_gain=ffn_in_gain, ffn_out_gain=ffn_out_gain, query_gain=query_gain, key_gain=key_gain)


eps = 1e-06
rope_base = 1000000.0

def dot_plain(left, right):
    return jnp.dot(left.astype(jnp.float32), right.astype(jnp.float32), preferred_element_type=jnp.float32)

def dot_last(left, right):
    return lax.dot_general(left.astype(jnp.float32), right.astype(jnp.float32), (((1,), (1,)), ((), ())), preferred_element_type=jnp.float32)

def dot_first(left, right):
    return lax.dot_general(left.astype(jnp.float32), right.astype(jnp.float32), (((0,), (0,)), ((), ())), preferred_element_type=jnp.float32)

def norm_parts(value):
    scale = lax.rsqrt(lax.optimization_barrier(jnp.mean(value * value, axis=-1, keepdims=True)) + eps)
    return (value * scale, scale)

def norm_back(dnormed, unit, scale):
    return scale * (dnormed - unit * lax.optimization_barrier(jnp.mean(dnormed * unit, axis=-1, keepdims=True)))

def rope_tables(position):
    freq = rope_base ** (-jnp.arange(HD // 2).astype(jnp.float32) * (2.0 / HD))
    angle = position.astype(jnp.float32)[:, None] * freq[None, :]
    return (jnp.cos(angle), jnp.sin(angle))

def rotate(value, cosine, sine):
    half = value.shape[-1] // 2
    first, second = (value[..., :half], value[..., half:])
    return jnp.concatenate([first * cosine - second * sine, second * cosine + first * sine], axis=-1)

def unrotate(value, cosine, sine):
    half = value.shape[-1] // 2
    first, second = (value[..., :half], value[..., half:])
    return jnp.concatenate([first * cosine + second * sine, second * cosine - first * sine], axis=-1)

def layout(lengths, count):
    index = jnp.arange(count).astype(jnp.int32)
    ends = jnp.cumsum(lengths).astype(jnp.int32)
    after = (index[:, None] >= ends[None, :]).astype(jnp.int32)
    segment = lax.optimization_barrier(jnp.sum(after, axis=1)).astype(jnp.int32)
    position = (index - lax.optimization_barrier(jnp.sum(after * lengths[None, :], axis=1))).astype(jnp.int32)
    return (segment, position)

def gelu_tanh(value):
    return jax.nn.gelu(value, approximate=True)

def reference(block_input, out_cotangent, seq_lengths, q_weight, k_weight, v_weight, o_weight, gate_weight, up_weight, down_weight, attn_in_gain, attn_out_gain, ffn_in_gain, ffn_out_gain, query_gain, key_gain):
    g_ai = attn_in_gain.astype(jnp.float32)
    g_ao = attn_out_gain.astype(jnp.float32)
    g_fi = ffn_in_gain.astype(jnp.float32)
    g_fo = ffn_out_gain.astype(jnp.float32)
    g_q = query_gain.astype(jnp.float32)
    g_k = key_gain.astype(jnp.float32)
    scaling = HD ** (-0.5)
    inputs = block_input.reshape(N_SHARD, LENGTH, D)
    cotangents = out_cotangent.reshape(N_SHARD, LENGTH, D)

    def one_row(carry, items):
        x_row, dy_row, lengths = items
        segment, position = layout(lengths, LENGTH)
        index = jnp.arange(LENGTH).astype(jnp.int32)
        allowed = (segment[:, None] == segment[None, :]) & (index[None, :] <= index[:, None])
        cosine, sine = rope_tables(position)
        unit1, r1 = norm_parts(x_row)
        xn1 = (unit1 * g_ai).astype(jnp.bfloat16)
        qp = dot_plain(xn1, q_weight).reshape(LENGTH, HEADS, HD)
        qunit, rq = norm_parts(qp)
        queries = rotate(qunit * g_q, cosine[:, None, :], sine[:, None, :]).astype(jnp.bfloat16)
        kp = dot_plain(xn1, k_weight)
        kunit, rk = norm_parts(kp)
        keys = rotate(kunit * g_k, cosine, sine).astype(jnp.bfloat16)
        values = dot_plain(xn1, v_weight).astype(jnp.bfloat16)

        def scores(query_head):
            raw = dot_last(query_head, keys) * scaling
            return jnp.where(allowed, raw, -1e+30)

        def head_forward(query_head):
            logits = scores(query_head)
            peak = lax.optimization_barrier(jnp.max(logits, axis=1, keepdims=True))
            lse = peak + jnp.log(lax.optimization_barrier(jnp.sum(jnp.exp(logits - peak), axis=1, keepdims=True)))
            weights = jnp.exp(logits - lse).astype(jnp.bfloat16)
            return (dot_plain(weights, values), lse)
        queries_t = jnp.transpose(queries, (1, 0, 2))
        head_out, lses = lax.map(head_forward, queries_t)
        attended = jnp.transpose(head_out, (1, 0, 2)).reshape(LENGTH, HEADS * HD).astype(jnp.bfloat16)
        proj = dot_last(attended, o_weight)
        aunit, ra = norm_parts(proj)
        h1 = x_row + aunit * g_ao
        unit2, r2 = norm_parts(h1)
        xn2 = (unit2 * g_fi).astype(jnp.bfloat16)
        gate = dot_plain(xn2, gate_weight)
        up = dot_plain(xn2, up_weight)
        act, gelu_back = jax.vjp(gelu_tanh, gate)
        hidden = (act * up).astype(jnp.bfloat16)
        ffn = dot_last(hidden, down_weight)
        funit, rf = norm_parts(ffn)
        out_row = h1 + funit * g_fo
        dg_fo = lax.optimization_barrier(jnp.sum(dy_row * funit, axis=0))
        dffn = norm_back(dy_row * g_fo, funit, rf).astype(jnp.bfloat16)
        dhid = dot_plain(dffn, down_weight)
        d_down = dot_first(dffn, hidden)
        dup = (dhid * act).astype(jnp.bfloat16)
        dgate = gelu_back(dhid * up)[0].astype(jnp.bfloat16)
        d_gate_w = dot_first(xn2, dgate)
        d_up_w = dot_first(xn2, dup)
        dxn2 = dot_last(dgate, gate_weight) + dot_last(dup, up_weight)
        dg_fi = lax.optimization_barrier(jnp.sum(dxn2 * unit2, axis=0))
        dh1 = dy_row + norm_back(dxn2 * g_fi, unit2, r2)
        dg_ao = lax.optimization_barrier(jnp.sum(dh1 * aunit, axis=0))
        dproj = norm_back(dh1 * g_ao, aunit, ra).astype(jnp.bfloat16)
        d_o_w = dot_first(dproj, attended)
        dattended = dot_plain(dproj, o_weight).astype(jnp.bfloat16)

        def head_backward(acc, items_head):
            query_head, out_head, dout_head, lse = items_head
            logits = scores(query_head)
            weights = jnp.exp(logits - lse)
            weights_low = weights.astype(jnp.bfloat16)
            delta = lax.optimization_barrier(jnp.sum(dout_head.astype(jnp.float32) * out_head.astype(jnp.float32), axis=1, keepdims=True))
            dprob = dot_last(dout_head, values)
            dscore = (weights * (dprob - delta) * scaling).astype(jnp.bfloat16)
            dq_head = dot_plain(dscore, keys)
            return ((acc[0] + dot_first(dscore, query_head), acc[1] + dot_first(weights_low, dout_head)), dq_head)
        out_t = jnp.transpose(attended.reshape(LENGTH, HEADS, HD), (1, 0, 2))
        dout_t = jnp.transpose(dattended.reshape(LENGTH, HEADS, HD), (1, 0, 2))
        start = (jnp.zeros((LENGTH, HD), jnp.float32), jnp.zeros((LENGTH, HD), jnp.float32))
        (dkeys, dvalues), dq_t = lax.scan(head_backward, start, (queries_t, out_t, dout_t, lses))
        dq = jnp.transpose(dq_t, (1, 0, 2))
        dqn = unrotate(dq, cosine[:, None, :], sine[:, None, :])
        dg_q = lax.optimization_barrier(jnp.sum(dqn * qunit, axis=(0, 1)))
        dqp = norm_back(dqn * g_q, qunit, rq).reshape(LENGTH, HEADS * HD).astype(jnp.bfloat16)
        dkn = unrotate(dkeys, cosine, sine)
        dg_k = lax.optimization_barrier(jnp.sum(dkn * kunit, axis=0))
        dkp = norm_back(dkn * g_k, kunit, rk).astype(jnp.bfloat16)
        dvr = dvalues.astype(jnp.bfloat16)
        dxn1 = dot_last(dqp, q_weight) + dot_last(dkp, k_weight) + dot_last(dvr, v_weight)
        d_q_w = dot_first(xn1, dqp)
        d_k_w = dot_first(xn1, dkp)
        d_v_w = dot_first(xn1, dvr)
        dg_ai = lax.optimization_barrier(jnp.sum(dxn1 * unit1, axis=0))
        dx_row = dh1 + norm_back(dxn1 * g_ai, unit1, r1)
        terms = (d_q_w, d_k_w, d_v_w, d_o_w, d_gate_w, d_up_w, d_down, dg_ai, dg_ao, dg_fi, dg_fo, dg_q, dg_k)
        carry = tuple((total + term for total, term in zip(carry, terms)))
        return (carry, (out_row, dx_row))
    shapes = [q_weight, k_weight, v_weight, o_weight, gate_weight, up_weight, down_weight, attn_in_gain, attn_out_gain, ffn_in_gain, ffn_out_gain, query_gain, key_gain]
    start = tuple((jnp.zeros(item.shape, jnp.float32) for item in shapes))
    grads, (outs, dxs) = lax.scan(one_row, start, (inputs, cotangents, seq_lengths))
    block_output = outs.reshape(TOKENS, D)
    input_grad = dxs.reshape(TOKENS, D)
    return (block_output, input_grad, grads[0], grads[1], grads[2], grads[3], grads[4], grads[5], grads[6], grads[7], grads[8], grads[9], grads[10], grads[11], grads[12])
```

```python
import functools

import jax
import jax.numpy as jnp
from jax import lax
from jax.experimental import pallas as pl
from jax.experimental.pallas import tpu as pltpu
from jax.sharding import PartitionSpec as P

HD = 256


eps = 1e-06
rope_base = 1000000.0


def dot_plain(left, right):
    return jnp.dot(left, right, preferred_element_type=jnp.float32)


def dot_last(left, right):
    return lax.dot_general(
        left, right, (((1,), (1,)), ((), ())), preferred_element_type=jnp.float32
    )


def dot_first(left, right):
    return lax.dot_general(
        left, right, (((0,), (0,)), ((), ())), preferred_element_type=jnp.float32
    )


def norm_parts(value):
    scale = lax.rsqrt(jnp.mean(value * value, axis=-1, keepdims=True) + eps)
    return (value * scale, scale)


def norm_back(dnormed, unit, scale):
    return scale * (dnormed - unit * jnp.mean(dnormed * unit, axis=-1, keepdims=True))


def rope_tables(position):
    freq = rope_base ** (-jnp.arange(HD // 2).astype(jnp.float32) * (2.0 / HD))
    angle = position.astype(jnp.float32)[:, None] * freq[None, :]
    return (jnp.cos(angle), jnp.sin(angle))


def rotate(value, cosine, sine):
    half = value.shape[-1] // 2
    first, second = (value[..., :half], value[..., half:])
    return jnp.concatenate(
        [first * cosine - second * sine, second * cosine + first * sine], axis=-1
    )


def unrotate(value, cosine, sine):
    half = value.shape[-1] // 2
    first, second = (value[..., :half], value[..., half:])
    return jnp.concatenate(
        [first * cosine + second * sine, second * cosine - first * sine], axis=-1
    )


def layout(lengths, count):
    index = jnp.arange(count)
    ends = jnp.cumsum(lengths)
    after = (index[:, None] >= ends[None, :]).astype(jnp.int32)
    segment = jnp.sum(after, axis=1)
    position = index - jnp.sum(after * lengths[None, :], axis=1)
    return (segment, position)


def gelu_tanh(value):
    return jax.nn.gelu(value, approximate=True)


def masked_scores(query_head, key_block, mask, scaling):
    raw = dot_last(query_head, key_block) * scaling
    return jnp.where(mask, raw, -1e30)

MESH = pl.DeviceIdType.MESH
LANES = 128
WAYS = 4


def vmem():
    return pl.BlockSpec(memory_space=pltpu.VMEM)


def greet(peers):
    barrier = pltpu.get_barrier_semaphore()
    for peer in peers:
        pl.semaphore_signal(barrier, inc=1, device_id=peer, device_id_type=MESH)
    pl.semaphore_wait(barrier, len(peers))


def params(number):
    return pltpu.CompilerParams(
        collective_id=number, has_side_effects=True, vmem_limit_bytes=56 * 1024 * 1024
    )


def send(src, dst, sems, where, peer):
    copy = pltpu.make_async_remote_copy(
        src_ref=src,
        dst_ref=dst,
        send_sem=sems[0].at[where],
        recv_sem=sems[1].at[where],
        device_id=peer,
        device_id_type=MESH,
    )
    copy.start()
    return copy


def place(n_ctx):
    shard, ctx, tp = (lax.axis_index("shard"), lax.axis_index("ctx"), lax.axis_index("tp"))
    core = lax.rem(ctx, 2)
    high = lax.rem(lax.div(ctx, 2), 2)
    return shard, ctx, tp, ctx + 1 - 2 * core, ctx + 2 - 4 * high


def columns(member, width):
    return pl.ds(pl.multiple_of(member * width, LANES), width)


def block_rows(index, count):
    return pl.ds(pl.multiple_of(index * count, 8), count)


def gather_kernel(n_shard, n_ctx, count, *refs):
    weights, unit, gain = (refs[:count], refs[count], refs[count + 1])
    refs = refs[count + 2 :]
    outs, row, gains = (refs[:count], refs[count], refs[count + 1])
    sems_a, sems_n, sems_f, sems_c, sems_x, sems_g, local = (
        refs[count + 2 : count + 4],
        refs[count + 4 : count + 6],
        refs[count + 6 : count + 8],
        refs[count + 8 : count + 10],
        refs[count + 10 : count + 12],
        refs[count + 12 : count + 14],
        refs[count + 14],
    )
    shard, ctx, tp, near, far = place(n_ctx)
    member = lax.rem(ctx, WAYS)
    rows = weights[0].shape[0]
    tokens = unit.shape[0]
    widths = [item.shape[1] // WAYS for item in weights]
    peers = [(lax.rem(shard + d, n_shard), ctx, tp) for d in range(1, n_shard)]
    mates = [(shard, lax.rem(ctx + d, n_ctx), tp) for d in range(1, n_ctx)]
    greet(peers + mates)
    started = []
    first = {}
    for d in range(1, n_shard):
        for a in range(count):
            cols = columns(member, widths[a])
            first[d, a] = send(
                weights[a].at[:, cols],
                outs[a].at[block_rows(shard, rows), cols],
                sems_a,
                (d - 1, a),
                peers[d - 1],
            )
        started.append(send(gain, gains.at[shard], sems_g, d - 1, peers[d - 1]))
    for d in range(1, n_ctx):
        started.append(
            send(unit, row.at[block_rows(ctx, tokens)], sems_x, d - 1, mates[d - 1])
        )
    own = [
        pltpu.make_async_copy(weights[a], outs[a].at[block_rows(shard, rows)], local.at[a])
        for a in range(count)
    ]
    own.append(pltpu.make_async_copy(unit, row.at[block_rows(ctx, tokens)], local.at[count]))
    own.append(pltpu.make_async_copy(gain, gains.at[shard], local.at[count + 1]))
    for item in own:
        item.start()
    across = {}
    for d in range(1, n_shard):
        source = lax.rem(shard - d + n_shard, n_shard)
        for a in range(count):
            first[d, a].wait_recv()
            block = outs[a].at[block_rows(source, rows), columns(member, widths[a])]
            across[d, a] = send(block, block, sems_f, (d - 1, a), (shard, far, tp))
            started.append(send(block, block, sems_n, (d - 1, a), (shard, near, tp)))
    other = lax.rem(far, WAYS)
    for d in range(1, n_shard):
        source = lax.rem(shard - d + n_shard, n_shard)
        for a in range(count):
            across[d, a].wait_recv()
            block = outs[a].at[block_rows(source, rows), columns(other, widths[a])]
            started.append(send(block, block, sems_c, (d - 1, a), (shard, near, tp)))
    for item in started:
        item.wait()
    for item in list(first.values()) + list(across.values()):
        item.wait_send()
    for item in own:
        item.wait()


def gather_all(n_shard, n_ctx, weights, unit, gain):
    count = len(weights)
    grid = pltpu.SemaphoreType.DMA((n_shard - 1, count))
    return pl.pallas_call(
        functools.partial(gather_kernel, n_shard, n_ctx, count),
        out_shape=[
            jax.ShapeDtypeStruct((item.shape[0] * n_shard, item.shape[1]), item.dtype)
            for item in weights
        ]
        + [
            jax.ShapeDtypeStruct((unit.shape[0] * n_ctx, unit.shape[1]), unit.dtype),
            jax.ShapeDtypeStruct((n_shard,) + gain.shape, gain.dtype),
        ],
        in_specs=[vmem()] * (count + 2),
        out_specs=[vmem()] * (count + 2),
        scratch_shapes=[grid] * 8
        + [pltpu.SemaphoreType.DMA((n_ctx - 1,))] * 2
        + [pltpu.SemaphoreType.DMA((n_shard - 1,))] * 2
        + [pltpu.SemaphoreType.DMA((count + 2,))],
        compiler_params=params(0),
        name="gather_all",
    )(*weights, unit, gain)


def tp_kernel(n_tp, part, out, inbox, send_sem, recv_sem):
    shard, ctx, tp = (lax.axis_index("shard"), lax.axis_index("ctx"), lax.axis_index("tp"))
    peers = [(shard, ctx, lax.rem(tp + d, n_tp)) for d in range(1, n_tp)]
    greet(peers)
    copies = [
        send(part, inbox.at[d - 1], (send_sem, recv_sem), d - 1, peers[d - 1])
        for d in range(1, n_tp)
    ]
    total = part[...].astype(jnp.float32)
    for d in range(1, n_tp):
        copies[d - 1].wait_recv()
        total = total + inbox[d - 1].astype(jnp.float32)
    out[...] = total
    for copy in copies:
        copy.wait_send()


def tp_sum(value, n_tp, number):
    part = value.astype(jnp.bfloat16)
    return pl.pallas_call(
        functools.partial(tp_kernel, n_tp),
        out_shape=jax.ShapeDtypeStruct(part.shape, jnp.float32),
        in_specs=[vmem()],
        out_specs=vmem(),
        scratch_shapes=[
            pltpu.VMEM((n_tp - 1,) + part.shape, jnp.bfloat16),
            pltpu.SemaphoreType.DMA((n_tp - 1,)),
            pltpu.SemaphoreType.DMA((n_tp - 1,)),
        ],
        compiler_params=params(number),
        name=f"tp_sum{number}",
    )(part)


def ctx_kernel(n_ctx, part, out, inbox, send_sem, recv_sem):
    shard, ctx, tp = (lax.axis_index("shard"), lax.axis_index("ctx"), lax.axis_index("tp"))
    tokens = out.shape[0]
    peers = [(shard, lax.rem(ctx + d, n_ctx), tp) for d in range(1, n_ctx)]
    greet(peers)
    copies = [
        send(
            part.at[block_rows(peers[d - 1][1], tokens)],
            inbox.at[d - 1],
            (send_sem, recv_sem),
            d - 1,
            peers[d - 1],
        )
        for d in range(1, n_ctx)
    ]
    total = part[block_rows(ctx, tokens), :].astype(jnp.float32)
    for d in range(1, n_ctx):
        copies[d - 1].wait_recv()
        total = total + inbox[d - 1].astype(jnp.float32)
    out[...] = total
    for copy in copies:
        copy.wait_send()


def ctx_scatter(value, n_ctx, number):
    part = value.astype(jnp.bfloat16)
    piece = (part.shape[0] // n_ctx, part.shape[1])
    return pl.pallas_call(
        functools.partial(ctx_kernel, n_ctx),
        out_shape=jax.ShapeDtypeStruct(piece, jnp.float32),
        in_specs=[vmem()],
        out_specs=vmem(),
        scratch_shapes=[
            pltpu.VMEM((n_ctx - 1,) + piece, jnp.bfloat16),
            pltpu.SemaphoreType.DMA((n_ctx - 1,)),
            pltpu.SemaphoreType.DMA((n_ctx - 1,)),
        ],
        compiler_params=params(number),
        name=f"ctx_scatter{number}",
    )(part)


def grad_kernel(n_shard, n_ctx, n_tp, count, kv_at, *refs):
    grads, gain = (refs[:count], refs[count])
    refs = refs[count + 1 :]
    outs, gain_out = (refs[: count + 1], refs[count + 1])
    (half, away, inbox, mine, arrived, done, kv_in, groups_in, shared) = refs[
        count + 2 : count + 11
    ]
    (g_near, g_far, g_mid, g_shard, g_group, g_tp) = refs[count + 11 : count + 17]
    sems = refs[count + 17 :]
    pair = [(sems[2 * k], sems[2 * k + 1]) for k in range(len(sems) // 2)]
    s_core, s_far, s_shard, s_group, s_kv, s_share, s_gain, s_gz, s_gg, s_gt = pair
    shard, ctx, tp, near, far = place(n_ctx)
    n_groups = n_ctx // WAYS
    group = lax.div(ctx, WAYS)
    member, other = (lax.rem(ctx, WAYS), lax.rem(far, WAYS))
    beside = lax.rem(near, WAYS)
    opposite = beside + other - member
    rows = outs[0].shape[0]
    widths = [item.shape[1] // WAYS for item in grads]
    starts = [sum(widths[:a]) for a in range(count)]
    near_id, far_id = ((shard, near, tp), (shard, far, tp))
    z_ids = [(lax.rem(shard + d, n_shard), ctx, tp) for d in range(1, n_shard)]
    g_ids = [(shard, lax.rem(ctx + WAYS * d, n_ctx), tp) for d in range(1, n_groups)]
    t_ids = [(shard, ctx, lax.rem(tp + d, n_tp)) for d in range(1, n_tp)]
    greet([near_id, far_id] + z_ids + g_ids + t_ids)

    ends = []
    core = {}
    for slot, quarter in ((1, opposite), (0, beside)):
        for a in range(count):
            core[slot, a] = send(
                grads[a].at[:, columns(quarter, widths[a])],
                half.at[slot, :, pl.ds(starts[a], widths[a])],
                s_core,
                (slot, a),
                near_id,
            )
    gain_near = send(gain, g_near, s_gain, 0, near_id)
    order = list(range(1, n_shard)) + [0]
    targets = [lax.rem(shard + d, n_shard) for d in range(n_shard)]

    for a in range(count):
        core[1, a].wait_recv()
    over = {}
    for d in order:
        where = block_rows(targets[d], rows)
        for a in range(count):
            cols = pl.ds(starts[a], widths[a])
            total = half[1, where, cols].astype(jnp.float32) + grads[a][
                where, columns(other, widths[a])
            ].astype(jnp.float32)
            away[where, cols] = total.astype(jnp.bfloat16)
        over[d] = send(away.at[where], inbox.at[where], s_far, d, far_id)

    gain_near.wait_recv()
    g_mid[0] = gain[...] + g_near[...]
    gain_far = send(g_mid.at[0], g_far, s_gain, 1, far_id)

    for a in range(count):
        core[0, a].wait_recv()
    along = {}
    for d in order:
        where = block_rows(targets[d], rows)
        over[d].wait_recv()
        for a in range(count):
            cols = pl.ds(starts[a], widths[a])
            total = (
                half[0, where, cols].astype(jnp.float32)
                + grads[a][where, columns(member, widths[a])].astype(jnp.float32)
                + inbox[where, cols].astype(jnp.float32)
            )
            mine[where, cols] = total.astype(jnp.bfloat16)
        if d:
            along[d] = send(mine.at[where], arrived.at[d - 1], s_shard, d - 1, z_ids[d - 1])

    gain_far.wait_recv()
    g_shard[shard] = g_mid[0] + g_far[...]
    gz = [
        send(g_shard.at[shard], g_shard.at[shard], s_gz, d - 1, z_ids[d - 1])
        for d in range(1, n_shard)
    ]
    total = mine[block_rows(shard, rows), :].astype(jnp.float32)
    for d in range(1, n_shard):
        along[d].wait_recv()
        total = total + arrived[d - 1].astype(jnp.float32)
    if n_groups > 1:
        groups_in[group] = total.astype(jnp.bfloat16)
        moved = [
            send(groups_in.at[group], groups_in.at[group], s_group, d - 1, g_ids[d - 1])
            for d in range(1, n_groups)
        ]
        for item in moved:
            item.wait_recv()
        ends = ends + moved
        total = groups_in[0].astype(jnp.float32)
        for g in range(1, n_groups):
            total = total + groups_in[g].astype(jnp.float32)
    done[...] = total.astype(jnp.bfloat16)
    kv_cols = pl.ds(starts[kv_at], widths[kv_at])
    kvs = [
        send(done.at[:, kv_cols], kv_in.at[d - 1], s_kv, d - 1, t_ids[d - 1])
        for d in range(1, n_tp)
    ]
    for item in gz:
        item.wait_recv()
    total = g_shard[0]
    for k in range(1, n_shard):
        total = total + g_shard[k]
    g_group[group] = total
    gg = [
        send(g_group.at[group], g_group.at[group], s_gg, d - 1, g_ids[d - 1])
        for d in range(1, n_groups)
    ]
    for item in gg:
        item.wait_recv()
    total = g_group[0]
    for k in range(1, n_groups):
        total = total + g_group[k]
    g_tp[tp] = total
    gt = [
        send(g_tp.at[tp], g_tp.at[tp], s_gt, d - 1, t_ids[d - 1]) for d in range(1, n_tp)
    ]

    shared[member] = done[...]
    total = done[:, kv_cols].astype(jnp.float32)
    for d in range(1, n_tp):
        kvs[d - 1].wait_recv()
        total = total + kv_in[d - 1].astype(jnp.float32)
    shared[member, :, kv_cols] = total.astype(jnp.bfloat16)
    piece = shared.at[member]
    to_far = send(piece, piece, s_share, 0, far_id)
    to_near = send(piece, piece, s_share, 1, near_id)
    to_far.wait_recv()
    piece = shared.at[other]
    relay = send(piece, piece, s_share, 2, near_id)
    for item in gt:
        item.wait_recv()
    total = g_tp[0]
    for k in range(1, n_tp):
        total = total + g_tp[k]
    gain_out[...] = total
    to_near.wait_recv()
    relay.wait_recv()
    for q in range(WAYS):
        for a in range(count):
            value = shared[q, :, pl.ds(starts[a], widths[a])].astype(jnp.float32)
            if a == kv_at:
                out = outs[a] if q < WAYS // 2 else outs[count]
                out[:, pl.ds((q % (WAYS // 2)) * widths[a], widths[a])] = value
            else:
                outs[a][:, pl.ds(q * widths[a], widths[a])] = value
    ends = ends + list(core.values()) + [gain_near, gain_far, to_far, to_near, relay]
    ends = ends + list(over.values()) + list(along.values()) + kvs + gz + gg + gt
    for item in ends:
        item.wait_send()


def reduce_grads(n_shard, n_ctx, n_tp, grads, kv_at, gain):
    count = len(grads)
    deep = grads[0].shape[0]
    rows = deep // n_shard
    n_groups = n_ctx // WAYS
    wide = sum([item.shape[1] // WAYS for item in grads])
    out_widths = [item.shape[1] for item in grads]
    out_widths[kv_at] = out_widths[kv_at] // 2
    out_widths.append(out_widths[kv_at])
    low, full = (jnp.bfloat16, jnp.float32)

    def dma(*shape):
        return [pltpu.SemaphoreType.DMA(shape)] * 2

    return pl.pallas_call(
        functools.partial(grad_kernel, n_shard, n_ctx, n_tp, count, kv_at),
        out_shape=[jax.ShapeDtypeStruct((rows, item), full) for item in out_widths]
        + [jax.ShapeDtypeStruct(gain.shape, full)],
        in_specs=[vmem()] * (count + 1),
        out_specs=[vmem()] * (count + 2),
        scratch_shapes=[
            pltpu.VMEM((2, deep, wide), low),
            pltpu.VMEM((deep, wide), low),
            pltpu.VMEM((deep, wide), low),
            pltpu.VMEM((deep, wide), low),
            pltpu.VMEM((n_shard - 1, rows, wide), low),
            pltpu.VMEM((rows, wide), low),
            pltpu.VMEM((n_tp - 1, rows, grads[kv_at].shape[1] // WAYS), low),
            pltpu.VMEM((n_groups, rows, wide), low),
            pltpu.VMEM((WAYS, rows, wide), low),
            pltpu.VMEM(gain.shape, full),
            pltpu.VMEM(gain.shape, full),
            pltpu.VMEM((1,) + gain.shape, full),
            pltpu.VMEM((n_shard,) + gain.shape, full),
            pltpu.VMEM((n_groups,) + gain.shape, full),
            pltpu.VMEM((n_tp,) + gain.shape, full),
        ]
        + dma(2, count)
        + dma(n_shard)
        + dma(n_shard - 1)
        + dma(max(n_groups - 1, 1))
        + dma(n_tp - 1)
        + dma(3)
        + dma(2)
        + dma(n_shard - 1)
        + dma(max(n_groups - 1, 1))
        + dma(n_tp - 1),
        compiler_params=params(6),
        name="reduce_grads",
    )(*grads, gain)


def pack_lanes(items):
    flat = jnp.concatenate([item.astype(jnp.float32) for item in items])
    unit = 8 * LANES
    short = -flat.shape[0] % unit
    return jnp.pad(flat, (0, short)).reshape(-1, LANES)


def per_device(
    block_input,
    out_cotangent,
    seq_lengths,
    q_weight,
    k_weight,
    v_weight,
    o_weight,
    gate_weight,
    up_weight,
    down_weight,
    attn_in_gain,
    attn_out_gain,
    ffn_in_gain,
    ffn_out_gain,
    query_gain,
    key_gain,
):
    tokens = block_input.shape[0]
    width = block_input.shape[1]
    n_ctx = lax.axis_size("ctx")
    n_tp = lax.axis_size("tp")
    row_len = tokens * n_ctx
    n_shard = lax.axis_size("shard")
    my_start = lax.axis_index("ctx") * tokens
    scaling = HD ** (-0.5)
    segment, position = layout(seq_lengths[0], row_len)
    key_index = jnp.arange(row_len)
    query_index = my_start + jnp.arange(tokens)
    query_seg = lax.dynamic_slice_in_dim(segment, my_start, tokens)
    allowed = (query_seg[:, None] == segment[None, :]) & (
        key_index[None, :] <= query_index[:, None]
    )
    row_cosine, row_sine = rope_tables(position)
    cosine = lax.dynamic_slice_in_dim(row_cosine, my_start, tokens)
    sine = lax.dynamic_slice_in_dim(row_sine, my_start, tokens)
    unit1, r1 = norm_parts(block_input)
    gains = (attn_in_gain, attn_out_gain, ffn_in_gain, ffn_out_gain, query_gain, key_gain)
    qw, kvw, ow, gw, uw, dw, unit_row, packed = gather_all(
        n_shard,
        n_ctx,
        (
            q_weight,
            jnp.concatenate([k_weight, v_weight], axis=1),
            o_weight,
            gate_weight,
            up_weight,
            down_weight,
        ),
        unit1.astype(jnp.bfloat16),
        pack_lanes(gains),
    )
    packed = packed.reshape(n_shard, -1)
    split = []
    at = 0
    for item in gains:
        split.append(packed[:, at : at + item.shape[0]].reshape(-1))
        at = at + item.shape[0]
    g_ai, g_ao, g_fi, g_fo, g_q, g_k = split
    local_heads = qw.shape[1] // HD
    xn1 = (unit1 * g_ai).astype(jnp.bfloat16)
    qp = dot_plain(xn1, qw).reshape(tokens, local_heads, HD)
    qunit, rq = norm_parts(qp)
    queries = rotate(qunit * g_q, cosine[:, None, :], sine[:, None, :]).astype(jnp.bfloat16)
    xn1_row = (unit_row.astype(jnp.float32) * g_ai).astype(jnp.bfloat16)
    kvp = dot_plain(xn1_row, kvw)
    row_kunit, row_rk = norm_parts(kvp[:, :HD])
    row_keys = rotate(row_kunit * g_k, row_cosine, row_sine).astype(jnp.bfloat16)
    row_values = kvp[:, HD:].astype(jnp.bfloat16)
    kunit = lax.dynamic_slice_in_dim(row_kunit, my_start, tokens)
    rk = lax.dynamic_slice_in_dim(row_rk, my_start, tokens)
    head_outs = []
    lses = []
    for head in range(local_heads):
        logits = masked_scores(queries[:, head, :], row_keys, allowed, scaling)
        peak = jnp.max(logits, axis=1, keepdims=True)
        lse = peak + jnp.log(jnp.sum(jnp.exp(logits - peak), axis=1, keepdims=True))
        weights = jnp.exp(logits - lse).astype(jnp.bfloat16)
        head_outs.append(dot_plain(weights, row_values))
        lses.append(lse)
    attended = jnp.concatenate(head_outs, axis=1).astype(jnp.bfloat16)
    proj = tp_sum(dot_last(attended, ow), n_tp, 1)
    aunit, ra = norm_parts(proj)
    h1 = block_input + aunit * g_ao
    unit2, r2 = norm_parts(h1)
    xn2 = (unit2 * g_fi).astype(jnp.bfloat16)
    gate = dot_plain(xn2, gw)
    up = dot_plain(xn2, uw)
    act, gelu_back = jax.vjp(gelu_tanh, gate)
    hidden = (act * up).astype(jnp.bfloat16)
    ffn = tp_sum(dot_last(hidden, dw), n_tp, 2)
    funit, rf = norm_parts(ffn)
    block_output = h1 + funit * g_fo
    back_keys, back_values = (row_keys, row_values)
    dg_fo = jnp.sum(out_cotangent * funit, axis=0)
    dffn = norm_back(out_cotangent * g_fo, funit, rf).astype(jnp.bfloat16)
    dhid = dot_plain(dffn, dw)
    d_down = dot_first(dffn, hidden)
    dup = (dhid * act).astype(jnp.bfloat16)
    dgate = gelu_back(dhid * up)[0].astype(jnp.bfloat16)
    d_gate_w = dot_first(xn2, dgate)
    d_up_w = dot_first(xn2, dup)
    dxn2 = tp_sum(dot_last(dgate, gw) + dot_last(dup, uw), n_tp, 3)
    dg_fi = jnp.sum(dxn2 * unit2, axis=0)
    dh1 = out_cotangent + norm_back(dxn2 * g_fi, unit2, r2)
    dg_ao = jnp.sum(dh1 * aunit, axis=0)
    dproj = norm_back(dh1 * g_ao, aunit, ra).astype(jnp.bfloat16)
    d_o_w = dot_first(dproj, attended)
    dattended = dot_plain(dproj, ow).astype(jnp.bfloat16)
    win_keys, win_values, win_allowed = (back_keys, back_values, allowed)
    key_terms = jnp.zeros((row_len, HD), jnp.float32)
    value_terms = jnp.zeros((row_len, HD), jnp.float32)
    dq_parts = []
    for head in range(local_heads):
        query_head = queries[:, head, :]
        out_head = attended[:, head * HD : (head + 1) * HD]
        dout_head = dattended[:, head * HD : (head + 1) * HD]
        logits = masked_scores(query_head, win_keys, win_allowed, scaling)
        weights = jnp.exp(logits - lses[head])
        weights_low = weights.astype(jnp.bfloat16)
        delta = jnp.sum(
            dout_head.astype(jnp.float32) * out_head.astype(jnp.float32), axis=1, keepdims=True
        )
        dprob = dot_last(dout_head, win_values)
        dscore = (weights * (dprob - delta) * scaling).astype(jnp.bfloat16)
        dq_parts.append(dot_plain(dscore, win_keys))
        key_terms = key_terms + dot_first(dscore, query_head)
        value_terms = value_terms + dot_first(weights_low, dout_head)
    dq = jnp.stack(dq_parts, axis=1)
    dqn = unrotate(dq, cosine[:, None, :], sine[:, None, :])
    dg_q = jnp.sum(dqn * qunit, axis=(0, 1))
    dqp = norm_back(dqn * g_q, qunit, rq).reshape(tokens, local_heads * HD).astype(jnp.bfloat16)
    dkv = ctx_scatter(jnp.concatenate([key_terms, value_terms], axis=1), n_ctx, 4)
    dkn = unrotate(dkv[:, :HD], cosine, sine)
    dg_k = jnp.sum(dkn * kunit, axis=0)
    dkp = norm_back(dkn * g_k, kunit, rk).astype(jnp.bfloat16)
    dkvp = jnp.concatenate([dkp, dkv[:, HD:].astype(jnp.bfloat16)], axis=1)
    dxn1 = tp_sum(dot_last(dqp, qw) + dot_last(dkvp, kvw), n_tp, 5)
    d_q_w = dot_first(xn1, dqp)
    d_kv_w = dot_first(xn1, dkvp)
    dg_ai = jnp.sum(dxn1 * unit1, axis=0)
    input_grad = dh1 + norm_back(dxn1 * g_ai, unit1, r1)
    low = [
        item.astype(jnp.bfloat16) for item in (d_q_w, d_kv_w, d_o_w, d_gate_w, d_up_w, d_down)
    ]
    share = 1.0 / n_tp
    gain_terms = (dg_ai * share, dg_ao * share, dg_fi * share, dg_fo * share, dg_q, dg_k)
    q_out, k_out, o_out, gate_out, up_out, down_out, v_out, gain_sums = reduce_grads(
        n_shard, n_ctx, n_tp, low, 1, pack_lanes(gain_terms)
    )
    flat = gain_sums.reshape(-1)
    gain_outs = []
    at = 0
    for term in gain_terms:
        own = term.shape[0] // n_shard
        gain_outs.append(
            lax.dynamic_slice_in_dim(flat, at + lax.axis_index("shard") * own, own)
        )
        at = at + term.shape[0]
    return (
        block_output,
        input_grad,
        q_out,
        k_out,
        v_out,
        o_out,
        gate_out,
        up_out,
        down_out,
        *gain_outs,
    )


def solution(mesh):
    placed = (
        P(("shard", "ctx"), None),
        P(("shard", "ctx"), None),
        P("shard", None),
        P("shard", "tp"),
        P("shard", None),
        P("shard", None),
        P("shard", "tp"),
        P("shard", "tp"),
        P("shard", "tp"),
        P("shard", "tp"),
        P("shard"),
        P("shard"),
        P("shard"),
        P("shard"),
        P("shard"),
        P("shard"),
    )
    return jax.shard_map(
        per_device,
        mesh=mesh,
        in_specs=placed,
        out_specs=(
            P(("shard", "ctx"), None),
            P(("shard", "ctx"), None),
            P("shard", "tp"),
            P("shard", None),
            P("shard", None),
            P("shard", "tp"),
            P("shard", "tp"),
            P("shard", "tp"),
            P("shard", "tp"),
            P("shard"),
            P("shard"),
            P("shard"),
            P("shard"),
            P("shard"),
            P("shard"),
        ),
        check_vma=False,
    )
```

```python
import functools

import jax
import jax.numpy as jnp
from jax import lax
from jax.experimental import pallas as pl
from jax.experimental.pallas import tpu as pltpu
from jax.sharding import PartitionSpec as P

HD = 256


eps = 1e-06
rope_base = 1000000.0


def dot_plain(left, right):
    return jnp.dot(left, right, preferred_element_type=jnp.float32)


def dot_last(left, right):
    return lax.dot_general(
        left, right, (((1,), (1,)), ((), ())), preferred_element_type=jnp.float32
    )


def dot_first(left, right):
    return lax.dot_general(
        left, right, (((0,), (0,)), ((), ())), preferred_element_type=jnp.float32
    )


def norm_parts(value):
    scale = lax.rsqrt(jnp.mean(value * value, axis=-1, keepdims=True) + eps)
    return (value * scale, scale)


def norm_back(dnormed, unit, scale):
    return scale * (dnormed - unit * jnp.mean(dnormed * unit, axis=-1, keepdims=True))


def rope_tables(position):
    freq = rope_base ** (-jnp.arange(HD // 2).astype(jnp.float32) * (2.0 / HD))
    angle = position.astype(jnp.float32)[:, None] * freq[None, :]
    return (jnp.cos(angle), jnp.sin(angle))


def rotate(value, cosine, sine):
    half = value.shape[-1] // 2
    first, second = (value[..., :half], value[..., half:])
    return jnp.concatenate(
        [first * cosine - second * sine, second * cosine + first * sine], axis=-1
    )


def unrotate(value, cosine, sine):
    half = value.shape[-1] // 2
    first, second = (value[..., :half], value[..., half:])
    return jnp.concatenate(
        [first * cosine + second * sine, second * cosine - first * sine], axis=-1
    )


def layout(lengths, count):
    index = jnp.arange(count)
    ends = jnp.cumsum(lengths)
    after = (index[:, None] >= ends[None, :]).astype(jnp.int32)
    segment = jnp.sum(after, axis=1)
    position = index - jnp.sum(after * lengths[None, :], axis=1)
    return (segment, position)


def gelu_tanh(value):
    return jax.nn.gelu(value, approximate=True)


def masked_scores(query_head, key_block, mask, scaling):
    raw = dot_last(query_head, key_block) * scaling
    return jnp.where(mask, raw, -1e30)

MESH = pl.DeviceIdType.MESH
LANES = 128
WAYS = 4


def vmem():
    return pl.BlockSpec(memory_space=pltpu.VMEM)


def greet(peers):
    barrier = pltpu.get_barrier_semaphore()
    for peer in peers:
        pl.semaphore_signal(barrier, inc=1, device_id=peer, device_id_type=MESH)
    pl.semaphore_wait(barrier, len(peers))


def params(number):
    return pltpu.CompilerParams(
        collective_id=number, has_side_effects=True, vmem_limit_bytes=56 * 1024 * 1024
    )


def send(src, dst, sems, where, peer):
    copy = pltpu.make_async_remote_copy(
        src_ref=src,
        dst_ref=dst,
        send_sem=sems[0].at[where],
        recv_sem=sems[1].at[where],
        device_id=peer,
        device_id_type=MESH,
    )
    copy.start()
    return copy


def place(n_ctx):
    shard, ctx, tp = (lax.axis_index("shard"), lax.axis_index("ctx"), lax.axis_index("tp"))
    core = lax.rem(ctx, 2)
    high = lax.rem(lax.div(ctx, 2), 2)
    return shard, ctx, tp, ctx + 1 - 2 * core, ctx + 2 - 4 * high


def columns(member, width):
    return pl.ds(pl.multiple_of(member * width, LANES), width)


def block_rows(index, count):
    return pl.ds(pl.multiple_of(index * count, 8), count)


def gather_kernel(n_shard, n_ctx, count, *refs):
    weights, unit, gain = (refs[:count], refs[count], refs[count + 1])
    refs = refs[count + 2 :]
    outs, row, gains = (refs[:count], refs[count], refs[count + 1])
    sems_a, sems_n, sems_f, sems_c, sems_x, sems_g, local = (
        refs[count + 2 : count + 4],
        refs[count + 4 : count + 6],
        refs[count + 6 : count + 8],
        refs[count + 8 : count + 10],
        refs[count + 10 : count + 12],
        refs[count + 12 : count + 14],
        refs[count + 14],
    )
    shard, ctx, tp, near, far = place(n_ctx)
    member = lax.rem(ctx, WAYS)
    rows = weights[0].shape[0]
    tokens = unit.shape[0]
    widths = [item.shape[1] // WAYS for item in weights]
    peers = [(lax.rem(shard + d, n_shard), ctx, tp) for d in range(1, n_shard)]
    mates = [(shard, lax.rem(ctx + d, n_ctx), tp) for d in range(1, n_ctx)]
    greet(peers + mates)
    started = []
    first = {}
    for d in range(1, n_shard):
        for a in range(count):
            cols = columns(member, widths[a])
            first[d, a] = send(
                weights[a].at[:, cols],
                outs[a].at[block_rows(shard, rows), cols],
                sems_a,
                (d - 1, a),
                peers[d - 1],
            )
        started.append(send(gain, gains.at[shard], sems_g, d - 1, peers[d - 1]))
    for d in range(1, n_ctx):
        started.append(
            send(unit, row.at[block_rows(ctx, tokens)], sems_x, d - 1, mates[d - 1])
        )
    own = [
        pltpu.make_async_copy(weights[a], outs[a].at[block_rows(shard, rows)], local.at[a])
        for a in range(count)
    ]
    own.append(pltpu.make_async_copy(unit, row.at[block_rows(ctx, tokens)], local.at[count]))
    own.append(pltpu.make_async_copy(gain, gains.at[shard], local.at[count + 1]))
    for item in own:
        item.start()
    across = {}
    for d in range(1, n_shard):
        source = lax.rem(shard - d + n_shard, n_shard)
        for a in range(count):
            first[d, a].wait_recv()
            block = outs[a].at[block_rows(source, rows), columns(member, widths[a])]
            across[d, a] = send(block, block, sems_f, (d - 1, a), (shard, far, tp))
            started.append(send(block, block, sems_n, (d - 1, a), (shard, near, tp)))
    other = lax.rem(far, WAYS)
    for d in range(1, n_shard):
        source = lax.rem(shard - d + n_shard, n_shard)
        for a in range(count):
            across[d, a].wait_recv()
            block = outs[a].at[block_rows(source, rows), columns(other, widths[a])]
            started.append(send(block, block, sems_c, (d - 1, a), (shard, near, tp)))
    for item in started:
        item.wait()
    for item in list(first.values()) + list(across.values()):
        item.wait_send()
    for item in own:
        item.wait()


def gather_all(n_shard, n_ctx, weights, unit, gain):
    count = len(weights)
    grid = pltpu.SemaphoreType.DMA((n_shard - 1, count))
    return pl.pallas_call(
        functools.partial(gather_kernel, n_shard, n_ctx, count),
        out_shape=[
            jax.ShapeDtypeStruct((item.shape[0] * n_shard, item.shape[1]), item.dtype)
            for item in weights
        ]
        + [
            jax.ShapeDtypeStruct((unit.shape[0] * n_ctx, unit.shape[1]), unit.dtype),
            jax.ShapeDtypeStruct((n_shard,) + gain.shape, gain.dtype),
        ],
        in_specs=[vmem()] * (count + 2),
        out_specs=[vmem()] * (count + 2),
        scratch_shapes=[grid] * 8
        + [pltpu.SemaphoreType.DMA((n_ctx - 1,))] * 2
        + [pltpu.SemaphoreType.DMA((n_shard - 1,))] * 2
        + [pltpu.SemaphoreType.DMA((count + 2,))],
        compiler_params=params(0),
        name="gather_all",
    )(*weights, unit, gain)


def tp_kernel(n_tp, part, out, inbox, send_sem, recv_sem):
    shard, ctx, tp = (lax.axis_index("shard"), lax.axis_index("ctx"), lax.axis_index("tp"))
    peers = [(shard, ctx, lax.rem(tp + d, n_tp)) for d in range(1, n_tp)]
    greet(peers)
    copies = [
        send(part, inbox.at[d - 1], (send_sem, recv_sem), d - 1, peers[d - 1])
        for d in range(1, n_tp)
    ]
    total = part[...].astype(jnp.float32)
    for d in range(1, n_tp):
        copies[d - 1].wait_recv()
        total = total + inbox[d - 1].astype(jnp.float32)
    out[...] = total
    for copy in copies:
        copy.wait_send()


def tp_sum(value, n_tp, number):
    part = value.astype(jnp.bfloat16)
    return pl.pallas_call(
        functools.partial(tp_kernel, n_tp),
        out_shape=jax.ShapeDtypeStruct(part.shape, jnp.float32),
        in_specs=[vmem()],
        out_specs=vmem(),
        scratch_shapes=[
            pltpu.VMEM((n_tp - 1,) + part.shape, jnp.bfloat16),
            pltpu.SemaphoreType.DMA((n_tp - 1,)),
            pltpu.SemaphoreType.DMA((n_tp - 1,)),
        ],
        compiler_params=params(number),
        name=f"tp_sum{number}",
    )(part)


def tail_kernel(n_shard, n_ctx, n_tp, early, *refs):
    ready = refs[:early]
    (terms, dqp, qw, kvw, xn1_t, cosine, sine, kunit, rk, g_k, unit1, r1, g_ai, dh1, gain) = refs[
        early : early + 15
    ]
    refs = refs[early + 15 :]
    count = early + 2
    kv_at = count - 1
    outs, gain_out, input_grad = (refs[: count + 1], refs[count + 1], refs[count + 2])
    (late_q, late_kv, dkv_in, part, part_in) = refs[count + 3 : count + 8]
    (half, away, inbox, mine, arrived, done, kv_in, groups_in, shared) = refs[
        count + 8 : count + 17
    ]
    (g_own, g_near, g_far, g_mid, g_shard, g_group, g_tp) = refs[count + 17 : count + 24]
    sems = refs[count + 24 :]
    pair = [(sems[2 * k], sems[2 * k + 1]) for k in range(len(sems) // 2)]
    (
        s_core,
        s_far,
        s_shard,
        s_group,
        s_kv,
        s_share,
        s_gain,
        s_gz,
        s_gg,
        s_gt,
        s_dkv,
        s_part,
    ) = pair
    grads = list(ready) + [late_q, late_kv]
    shard, ctx, tp, near, far = place(n_ctx)
    n_groups = n_ctx // WAYS
    group = lax.div(ctx, WAYS)
    member, other = (lax.rem(ctx, WAYS), lax.rem(far, WAYS))
    beside = lax.rem(near, WAYS)
    opposite = beside + other - member
    rows = outs[0].shape[0]
    tokens = dqp.shape[0]
    widths = [item.shape[1] // WAYS for item in grads]
    starts = [sum(widths[:a]) for a in range(count)]
    batches = (list(range(early)), [early, early + 1])
    spans = (
        pl.ds(0, starts[early]),
        pl.ds(starts[early], widths[early] + widths[early + 1]),
    )
    near_id, far_id = ((shard, near, tp), (shard, far, tp))
    z_ids = [(lax.rem(shard + d, n_shard), ctx, tp) for d in range(1, n_shard)]
    c_ids = [(shard, lax.rem(ctx + d, n_ctx), tp) for d in range(1, n_ctx)]
    g_ids = [(shard, lax.rem(ctx + WAYS * d, n_ctx), tp) for d in range(1, n_groups)]
    t_ids = [(shard, ctx, lax.rem(tp + d, n_tp)) for d in range(1, n_tp)]
    greet(z_ids + c_ids + t_ids)

    ends = []
    core = {}
    over = {}
    along = {}
    order = list(range(1, n_shard)) + [0]
    targets = [lax.rem(shard + d, n_shard) for d in range(n_shard)]

    def start_core(batch):
        for slot, quarter in ((1, opposite), (0, beside)):
            for a in batches[batch]:
                core[slot, a] = send(
                    grads[a].at[:, columns(quarter, widths[a])],
                    half.at[slot, :, pl.ds(starts[a], widths[a])],
                    s_core,
                    (slot, a),
                    near_id,
                )

    def start_over(batch):
        for a in batches[batch]:
            core[1, a].wait_recv()
        for d in order:
            where = block_rows(targets[d], rows)
            for a in batches[batch]:
                cols = pl.ds(starts[a], widths[a])
                total = half[1, where, cols].astype(jnp.float32) + grads[a][
                    where, columns(other, widths[a])
                ].astype(jnp.float32)
                away[where, cols] = total.astype(jnp.bfloat16)
            over[batch, d] = send(
                away.at[where, spans[batch]],
                inbox.at[where, spans[batch]],
                s_far,
                (batch, d),
                far_id,
            )

    def start_along(batch):
        for a in batches[batch]:
            core[0, a].wait_recv()
        for d in order:
            where = block_rows(targets[d], rows)
            over[batch, d].wait_recv()
            for a in batches[batch]:
                cols = pl.ds(starts[a], widths[a])
                total = (
                    half[0, where, cols].astype(jnp.float32)
                    + grads[a][where, columns(member, widths[a])].astype(jnp.float32)
                    + inbox[where, cols].astype(jnp.float32)
                )
                mine[where, cols] = total.astype(jnp.bfloat16)
            if d:
                along[batch, d] = send(
                    mine.at[where, spans[batch]],
                    arrived.at[d - 1, :, spans[batch]],
                    s_shard,
                    (batch, d - 1),
                    z_ids[d - 1],
                )

    def finish(batch):
        span = spans[batch]
        total = mine[block_rows(shard, rows), span].astype(jnp.float32)
        for d in range(1, n_shard):
            along[batch, d].wait_recv()
            total = total + arrived[d - 1, :, span].astype(jnp.float32)
        if n_groups > 1:
            groups_in[group, :, span] = total.astype(jnp.bfloat16)
            piece = groups_in.at[group, :, span]
            moved = [
                send(piece, piece, s_group, (batch, d - 1), g_ids[d - 1])
                for d in range(1, n_groups)
            ]
            for item in moved:
                item.wait_recv()
            ends.extend(moved)
            total = groups_in[0, :, span].astype(jnp.float32)
            for g in range(1, n_groups):
                total = total + groups_in[g, :, span].astype(jnp.float32)
        return total.astype(jnp.bfloat16)

    def start_share(batch):
        piece = shared.at[member, :, spans[batch]]
        return (
            send(piece, piece, s_share, (batch, 0), far_id),
            send(piece, piece, s_share, (batch, 1), near_id),
        )

    def relay_share(batch, first):
        first[0].wait_recv()
        piece = shared.at[other, :, spans[batch]]
        return send(piece, piece, s_share, (batch, 2), near_id)

    scatter = [
        send(
            terms.at[block_rows(c_ids[d - 1][1], tokens)],
            dkv_in.at[d - 1],
            s_dkv,
            d - 1,
            c_ids[d - 1],
        )
        for d in range(1, n_ctx)
    ]
    start_core(0)
    late_q[...] = dot_plain(xn1_t[...], dqp[...]).astype(jnp.bfloat16)
    dxn1 = dot_last(dqp[...], qw[...])
    dkv = terms[block_rows(ctx, tokens), :].astype(jnp.float32)
    for d in range(1, n_ctx):
        scatter[d - 1].wait_recv()
        dkv = dkv + dkv_in[d - 1].astype(jnp.float32)
    dkn = unrotate(dkv[:, :HD], cosine[...], sine[...])
    dg_k = jnp.sum(dkn * kunit[...], axis=0, keepdims=True)
    dkp = norm_back(dkn * g_k[...], kunit[...], rk[...]).astype(jnp.bfloat16)
    dkvp = jnp.concatenate([dkp, dkv[:, HD:].astype(jnp.bfloat16)], axis=1)
    part[...] = (dxn1 + dot_last(dkvp, kvw[...])).astype(jnp.bfloat16)
    parts = [
        send(part, part_in.at[d - 1], s_part, d - 1, t_ids[d - 1]) for d in range(1, n_tp)
    ]
    late_kv[...] = dot_plain(xn1_t[...], dkvp).astype(jnp.bfloat16)
    start_over(0)
    start_core(1)
    dxn1 = part[...].astype(jnp.float32)
    for d in range(1, n_tp):
        parts[d - 1].wait_recv()
        dxn1 = dxn1 + part_in[d - 1].astype(jnp.float32)
    dg_ai = jnp.sum(dxn1 * unit1[...], axis=0, keepdims=True) * (1.0 / n_tp)
    input_grad[...] = dh1[...] + norm_back(dxn1 * g_ai[...], unit1[...], r1[...])
    g_own[...] = gain[...]
    at = 0
    for line in (dg_ai, dg_k):
        for k in range(line.shape[1] // LANES):
            g_own[pl.ds(at, 1), :] = line[:, k * LANES : (k + 1) * LANES]
            at = at + 1
    gain_near = send(g_own, g_near, s_gain, 0, near_id)
    start_over(1)
    gain_near.wait_recv()
    g_mid[0] = g_own[...] + g_near[...]
    gain_far = send(g_mid.at[0], g_far, s_gain, 1, far_id)

    start_along(0)
    gain_far.wait_recv()
    g_shard[shard] = g_mid[0] + g_far[...]
    gz = [
        send(g_shard.at[shard], g_shard.at[shard], s_gz, d - 1, z_ids[d - 1])
        for d in range(1, n_shard)
    ]
    start_along(1)
    shared[member, :, spans[0]] = finish(0)
    share0 = start_share(0)

    for item in gz:
        item.wait_recv()
    total = g_shard[0]
    for k in range(1, n_shard):
        total = total + g_shard[k]
    g_group[group] = total
    gg = [
        send(g_group.at[group], g_group.at[group], s_gg, d - 1, g_ids[d - 1])
        for d in range(1, n_groups)
    ]
    for item in gg:
        item.wait_recv()
    total = g_group[0]
    for k in range(1, n_groups):
        total = total + g_group[k]
    g_tp[tp] = total
    gt = [
        send(g_tp.at[tp], g_tp.at[tp], s_gt, d - 1, t_ids[d - 1]) for d in range(1, n_tp)
    ]

    done[...] = finish(1)
    kv_cols = pl.ds(widths[early], widths[kv_at])
    kvs = [
        send(done.at[:, kv_cols], kv_in.at[d - 1], s_kv, d - 1, t_ids[d - 1])
        for d in range(1, n_tp)
    ]
    relay0 = relay_share(0, share0)
    shared[member, :, pl.ds(starts[early], widths[early])] = done[:, pl.ds(0, widths[early])]
    total = done[:, kv_cols].astype(jnp.float32)
    for d in range(1, n_tp):
        kvs[d - 1].wait_recv()
        total = total + kv_in[d - 1].astype(jnp.float32)
    shared[member, :, pl.ds(starts[kv_at], widths[kv_at])] = total.astype(jnp.bfloat16)
    share1 = start_share(1)
    for item in gt:
        item.wait_recv()
    total = g_tp[0]
    for k in range(1, n_tp):
        total = total + g_tp[k]
    gain_out[...] = total

    def write(batch):
        for q in range(WAYS):
            for a in batches[batch]:
                value = shared[q, :, pl.ds(starts[a], widths[a])]
                if a == kv_at:
                    out = outs[a] if q < WAYS // 2 else outs[count]
                    out[:, pl.ds((q % (WAYS // 2)) * widths[a], widths[a])] = value
                else:
                    outs[a][:, pl.ds(q * widths[a], widths[a])] = value

    share0[1].wait_recv()
    relay0.wait_recv()
    write(0)
    relay1 = relay_share(1, share1)
    share1[1].wait_recv()
    relay1.wait_recv()
    write(1)
    ends.extend(scatter + parts + list(core.values()) + list(over.values()))
    ends.extend(list(along.values()) + kvs + gz + gg + gt + [gain_near, gain_far])
    ends.extend(list(share0) + list(share1) + [relay0, relay1])
    for item in ends:
        item.wait_send()


def run_tail(n_shard, n_ctx, n_tp, ready, terms, dqp, qw, kvw, xn1_t, small, dh1, gain):
    deep = qw.shape[0]
    tokens = dqp.shape[0]
    rows = deep // n_shard
    n_groups = n_ctx // WAYS
    early = len(ready)
    count = early + 2
    late = (qw.shape[1], kvw.shape[1])
    wide = sum([item.shape[1] // WAYS for item in ready]) + sum(late) // WAYS
    out_widths = [item.shape[1] for item in ready] + [late[0], late[1] // 2, late[1] // 2]
    low, full = (jnp.bfloat16, jnp.float32)
    operands = (*ready, terms, dqp, qw, kvw, xn1_t, *small, dh1, gain)

    def dma(*shape):
        return [pltpu.SemaphoreType.DMA(shape)] * 2

    return pl.pallas_call(
        functools.partial(tail_kernel, n_shard, n_ctx, n_tp, early),
        out_shape=[jax.ShapeDtypeStruct((rows, item), low) for item in out_widths]
        + [jax.ShapeDtypeStruct(gain.shape, full), jax.ShapeDtypeStruct(dh1.shape, full)],
        in_specs=[vmem()] * len(operands),
        out_specs=[vmem()] * (count + 3),
        scratch_shapes=[
            pltpu.VMEM((deep, late[0]), low),
            pltpu.VMEM((deep, late[1]), low),
            pltpu.VMEM((n_ctx - 1, tokens, terms.shape[1]), low),
            pltpu.VMEM((tokens, deep), low),
            pltpu.VMEM((n_tp - 1, tokens, deep), low),
            pltpu.VMEM((2, deep, wide), low),
            pltpu.VMEM((deep, wide), low),
            pltpu.VMEM((deep, wide), low),
            pltpu.VMEM((deep, wide), low),
            pltpu.VMEM((n_shard - 1, rows, wide), low),
            pltpu.VMEM((rows, sum(late) // WAYS), low),
            pltpu.VMEM((n_tp - 1, rows, late[1] // WAYS), low),
            pltpu.VMEM((n_groups, rows, wide), low),
            pltpu.VMEM((WAYS, rows, wide), low),
            pltpu.VMEM(gain.shape, full),
            pltpu.VMEM(gain.shape, full),
            pltpu.VMEM(gain.shape, full),
            pltpu.VMEM((1,) + gain.shape, full),
            pltpu.VMEM((n_shard,) + gain.shape, full),
            pltpu.VMEM((n_groups,) + gain.shape, full),
            pltpu.VMEM((n_tp,) + gain.shape, full),
        ]
        + dma(2, count)
        + dma(2, n_shard)
        + dma(2, n_shard - 1)
        + dma(2, max(n_groups - 1, 1))
        + dma(n_tp - 1)
        + dma(2, 3)
        + dma(2)
        + dma(n_shard - 1)
        + dma(max(n_groups - 1, 1))
        + dma(n_tp - 1)
        + dma(n_ctx - 1)
        + dma(n_tp - 1),
        compiler_params=params(6),
        name="tail",
    )(*operands)


def pack_lanes(items):
    flat = jnp.concatenate([item.astype(jnp.float32) for item in items])
    unit = 8 * LANES
    short = -flat.shape[0] % unit
    return jnp.pad(flat, (0, short)).reshape(-1, LANES)


def per_device(
    block_input,
    out_cotangent,
    seq_lengths,
    q_weight,
    k_weight,
    v_weight,
    o_weight,
    gate_weight,
    up_weight,
    down_weight,
    attn_in_gain,
    attn_out_gain,
    ffn_in_gain,
    ffn_out_gain,
    query_gain,
    key_gain,
):
    tokens = block_input.shape[0]
    width = block_input.shape[1]
    n_ctx = lax.axis_size("ctx")
    n_tp = lax.axis_size("tp")
    row_len = tokens * n_ctx
    n_shard = lax.axis_size("shard")
    my_start = lax.axis_index("ctx") * tokens
    scaling = HD ** (-0.5)
    segment, position = layout(seq_lengths[0], row_len)
    key_index = jnp.arange(row_len)
    query_index = my_start + jnp.arange(tokens)
    query_seg = lax.dynamic_slice_in_dim(segment, my_start, tokens)
    allowed = (query_seg[:, None] == segment[None, :]) & (
        key_index[None, :] <= query_index[:, None]
    )
    row_cosine, row_sine = rope_tables(position)
    cosine = lax.dynamic_slice_in_dim(row_cosine, my_start, tokens)
    sine = lax.dynamic_slice_in_dim(row_sine, my_start, tokens)
    unit1, r1 = norm_parts(block_input)
    gains = (attn_in_gain, attn_out_gain, ffn_in_gain, ffn_out_gain, query_gain, key_gain)
    qw, kvw, ow, gw, uw, dw, unit_row, packed = gather_all(
        n_shard,
        n_ctx,
        (
            q_weight,
            jnp.concatenate([k_weight, v_weight], axis=1),
            o_weight,
            gate_weight,
            up_weight,
            down_weight,
        ),
        unit1.astype(jnp.bfloat16),
        pack_lanes(gains),
    )
    packed = packed.reshape(n_shard, -1)
    split = []
    at = 0
    for item in gains:
        split.append(packed[:, at : at + item.shape[0]].reshape(-1))
        at = at + item.shape[0]
    g_ai, g_ao, g_fi, g_fo, g_q, g_k = split
    local_heads = qw.shape[1] // HD
    xn1 = (unit1 * g_ai).astype(jnp.bfloat16)
    qp = dot_plain(xn1, qw).reshape(tokens, local_heads, HD)
    qunit, rq = norm_parts(qp)
    queries = rotate(qunit * g_q, cosine[:, None, :], sine[:, None, :]).astype(jnp.bfloat16)
    xn1_row = (unit_row.astype(jnp.float32) * g_ai).astype(jnp.bfloat16)
    kvp = dot_plain(xn1_row, kvw)
    row_kunit, row_rk = norm_parts(kvp[:, :HD])
    row_keys = rotate(row_kunit * g_k, row_cosine, row_sine).astype(jnp.bfloat16)
    row_values = kvp[:, HD:].astype(jnp.bfloat16)
    kunit = lax.dynamic_slice_in_dim(row_kunit, my_start, tokens)
    rk = lax.dynamic_slice_in_dim(row_rk, my_start, tokens)
    head_outs = []
    lses = []
    for head in range(local_heads):
        logits = masked_scores(queries[:, head, :], row_keys, allowed, scaling)
        peak = jnp.max(logits, axis=1, keepdims=True)
        lse = peak + jnp.log(jnp.sum(jnp.exp(logits - peak), axis=1, keepdims=True))
        weights = jnp.exp(logits - lse).astype(jnp.bfloat16)
        head_outs.append(dot_plain(weights, row_values))
        lses.append(lse)
    attended = jnp.concatenate(head_outs, axis=1).astype(jnp.bfloat16)
    proj = tp_sum(dot_last(attended, ow), n_tp, 1)
    aunit, ra = norm_parts(proj)
    h1 = block_input + aunit * g_ao
    unit2, r2 = norm_parts(h1)
    xn2 = (unit2 * g_fi).astype(jnp.bfloat16)
    gate = dot_plain(xn2, gw)
    up = dot_plain(xn2, uw)
    act, gelu_back = jax.vjp(gelu_tanh, gate)
    hidden = (act * up).astype(jnp.bfloat16)
    ffn = tp_sum(dot_last(hidden, dw), n_tp, 2)
    funit, rf = norm_parts(ffn)
    block_output = h1 + funit * g_fo
    back_keys, back_values = (row_keys, row_values)
    dg_fo = jnp.sum(out_cotangent * funit, axis=0)
    dffn = norm_back(out_cotangent * g_fo, funit, rf).astype(jnp.bfloat16)
    dhid = dot_plain(dffn, dw)
    d_down = dot_first(dffn, hidden)
    dup = (dhid * act).astype(jnp.bfloat16)
    dgate = gelu_back(dhid * up)[0].astype(jnp.bfloat16)
    d_gate_w = dot_first(xn2, dgate)
    d_up_w = dot_first(xn2, dup)
    dxn2 = tp_sum(dot_last(dgate, gw) + dot_last(dup, uw), n_tp, 3)
    dg_fi = jnp.sum(dxn2 * unit2, axis=0)
    dh1 = out_cotangent + norm_back(dxn2 * g_fi, unit2, r2)
    dg_ao = jnp.sum(dh1 * aunit, axis=0)
    dproj = norm_back(dh1 * g_ao, aunit, ra).astype(jnp.bfloat16)
    d_o_w = dot_first(dproj, attended)
    dattended = dot_plain(dproj, ow).astype(jnp.bfloat16)
    win_keys, win_values, win_allowed = (back_keys, back_values, allowed)
    key_terms = jnp.zeros((row_len, HD), jnp.float32)
    value_terms = jnp.zeros((row_len, HD), jnp.float32)
    dq_parts = []
    for head in range(local_heads):
        query_head = queries[:, head, :]
        out_head = attended[:, head * HD : (head + 1) * HD]
        dout_head = dattended[:, head * HD : (head + 1) * HD]
        logits = masked_scores(query_head, win_keys, win_allowed, scaling)
        weights = jnp.exp(logits - lses[head])
        weights_low = weights.astype(jnp.bfloat16)
        delta = jnp.sum(
            dout_head.astype(jnp.float32) * out_head.astype(jnp.float32), axis=1, keepdims=True
        )
        dprob = dot_last(dout_head, win_values)
        dscore = (weights * (dprob - delta) * scaling).astype(jnp.bfloat16)
        dq_parts.append(dot_plain(dscore, win_keys))
        key_terms = key_terms + dot_first(dscore, query_head)
        value_terms = value_terms + dot_first(weights_low, dout_head)
    dq = jnp.stack(dq_parts, axis=1)
    dqn = unrotate(dq, cosine[:, None, :], sine[:, None, :])
    dg_q = jnp.sum(dqn * qunit, axis=(0, 1))
    dqp = norm_back(dqn * g_q, qunit, rq).reshape(tokens, local_heads * HD).astype(jnp.bfloat16)
    terms = jnp.concatenate([key_terms, value_terms], axis=1).astype(jnp.bfloat16)
    ready = [item.astype(jnp.bfloat16) for item in (d_o_w, d_gate_w, d_up_w, d_down)]
    share = 1.0 / n_tp
    late = (jnp.zeros((width,), jnp.float32), jnp.zeros((HD,), jnp.float32))
    sums = (*late, dg_ao * share, dg_fi * share, dg_fo * share, dg_q)
    outs = run_tail(
        n_shard,
        n_ctx,
        n_tp,
        ready,
        terms,
        dqp,
        qw,
        kvw,
        xn1.T,
        (cosine, sine, kunit, rk, g_k[None, :], unit1, r1, g_ai[None, :]),
        dh1,
        pack_lanes(sums),
    )
    o_out, gate_out, up_out, down_out, q_out, k_out, v_out = [
        item.astype(jnp.float32) for item in outs[:7]
    ]
    gain_sums, input_grad = outs[7:]
    flat = gain_sums.reshape(-1)
    gain_outs = []
    at = 0
    for term in sums:
        own = term.shape[0] // n_shard
        gain_outs.append(
            lax.dynamic_slice_in_dim(flat, at + lax.axis_index("shard") * own, own)
        )
        at = at + term.shape[0]
    dg_ai, dg_k, dg_ao, dg_fi, dg_fo, dg_q = gain_outs
    return (
        block_output,
        input_grad,
        q_out,
        k_out,
        v_out,
        o_out,
        gate_out,
        up_out,
        down_out,
        dg_ai,
        dg_ao,
        dg_fi,
        dg_fo,
        dg_q,
        dg_k,
    )


def solution(mesh):
    placed = (
        P(("shard", "ctx"), None),
        P(("shard", "ctx"), None),
        P("shard", None),
        P("shard", "tp"),
        P("shard", None),
        P("shard", None),
        P("shard", "tp"),
        P("shard", "tp"),
        P("shard", "tp"),
        P("shard", "tp"),
        P("shard"),
        P("shard"),
        P("shard"),
        P("shard"),
        P("shard"),
        P("shard"),
    )
    return jax.shard_map(
        per_device,
        mesh=mesh,
        in_specs=placed,
        out_specs=(
            P(("shard", "ctx"), None),
            P(("shard", "ctx"), None),
            P("shard", "tp"),
            P("shard", None),
            P("shard", None),
            P("shard", "tp"),
            P("shard", "tp"),
            P("shard", "tp"),
            P("shard", "tp"),
            P("shard"),
            P("shard"),
            P("shard"),
            P("shard"),
            P("shard"),
            P("shard"),
        ),
        check_vma=False,
    )
```

```python
import functools

import jax
import jax.numpy as jnp
from jax import lax
from jax.experimental import pallas as pl
from jax.experimental.pallas import tpu as pltpu
from jax.sharding import PartitionSpec as P

HD = 256


eps = 1e-06
rope_base = 1000000.0


def dot_plain(left, right):
    return jnp.dot(left, right, preferred_element_type=jnp.float32)


def dot_last(left, right):
    return lax.dot_general(
        left, right, (((1,), (1,)), ((), ())), preferred_element_type=jnp.float32
    )


def dot_first(left, right):
    return lax.dot_general(
        left, right, (((0,), (0,)), ((), ())), preferred_element_type=jnp.float32
    )


def norm_parts(value):
    scale = lax.rsqrt(jnp.mean(value * value, axis=-1, keepdims=True) + eps)
    return (value * scale, scale)


def norm_back(dnormed, unit, scale):
    return scale * (dnormed - unit * jnp.mean(dnormed * unit, axis=-1, keepdims=True))


def rope_tables(position):
    freq = rope_base ** (-jnp.arange(HD // 2).astype(jnp.float32) * (2.0 / HD))
    angle = position.astype(jnp.float32)[:, None] * freq[None, :]
    return (jnp.cos(angle), jnp.sin(angle))


def rotate(value, cosine, sine):
    half = value.shape[-1] // 2
    first, second = (value[..., :half], value[..., half:])
    return jnp.concatenate(
        [first * cosine - second * sine, second * cosine + first * sine], axis=-1
    )


def unrotate(value, cosine, sine):
    half = value.shape[-1] // 2
    first, second = (value[..., :half], value[..., half:])
    return jnp.concatenate(
        [first * cosine + second * sine, second * cosine - first * sine], axis=-1
    )


def layout(lengths, count):
    index = jnp.arange(count)
    ends = jnp.cumsum(lengths)
    after = (index[:, None] >= ends[None, :]).astype(jnp.int32)
    segment = jnp.sum(after, axis=1)
    position = index - jnp.sum(after * lengths[None, :], axis=1)
    return (segment, position)


def gelu_tanh(value):
    return jax.nn.gelu(value, approximate=True)


def masked_scores(query_head, key_block, mask, scaling):
    raw = dot_last(query_head, key_block) * scaling
    return jnp.where(mask, raw, -1e30)

MESH = pl.DeviceIdType.MESH
LANES = 128
WAYS = 4


def vmem():
    return pl.BlockSpec(memory_space=pltpu.VMEM)


def greet(peers):
    barrier = pltpu.get_barrier_semaphore()
    for peer in peers:
        pl.semaphore_signal(barrier, inc=1, device_id=peer, device_id_type=MESH)
    pl.semaphore_wait(barrier, len(peers))


def params(number):
    return pltpu.CompilerParams(
        collective_id=number, has_side_effects=True, vmem_limit_bytes=56 * 1024 * 1024
    )


def send(src, dst, sems, where, peer):
    copy = pltpu.make_async_remote_copy(
        src_ref=src,
        dst_ref=dst,
        send_sem=sems[0].at[where],
        recv_sem=sems[1].at[where],
        device_id=peer,
        device_id_type=MESH,
    )
    copy.start()
    return copy


def place(n_ctx):
    shard, ctx, tp = (lax.axis_index("shard"), lax.axis_index("ctx"), lax.axis_index("tp"))
    core = lax.rem(ctx, 2)
    high = lax.rem(lax.div(ctx, 2), 2)
    return shard, ctx, tp, ctx + 1 - 2 * core, ctx + 2 - 4 * high


def columns(member, width):
    return pl.ds(pl.multiple_of(member * width, LANES), width)


def block_rows(index, count):
    return pl.ds(pl.multiple_of(index * count, 8), count)


def gather_kernel(n_shard, n_ctx, count, *refs):
    weights, unit, gain = (refs[:count], refs[count], refs[count + 1])
    refs = refs[count + 2 :]
    outs, row, gains = (refs[:count], refs[count], refs[count + 1])
    sems_a, sems_n, sems_f, sems_c, sems_x, sems_g, local = (
        refs[count + 2 : count + 4],
        refs[count + 4 : count + 6],
        refs[count + 6 : count + 8],
        refs[count + 8 : count + 10],
        refs[count + 10 : count + 12],
        refs[count + 12 : count + 14],
        refs[count + 14],
    )
    shard, ctx, tp, near, far = place(n_ctx)
    member = lax.rem(ctx, WAYS)
    rows = weights[0].shape[0]
    tokens = unit.shape[0]
    widths = [item.shape[1] // WAYS for item in weights]
    peers = [(lax.rem(shard + d, n_shard), ctx, tp) for d in range(1, n_shard)]
    mates = [(shard, lax.rem(ctx + d, n_ctx), tp) for d in range(1, n_ctx)]
    greet(peers + mates)
    started = []
    first = {}
    for d in range(1, n_shard):
        for a in range(count):
            cols = columns(member, widths[a])
            first[d, a] = send(
                weights[a].at[:, cols],
                outs[a].at[block_rows(shard, rows), cols],
                sems_a,
                (d - 1, a),
                peers[d - 1],
            )
        started.append(send(gain, gains.at[shard], sems_g, d - 1, peers[d - 1]))
    for d in range(1, n_ctx):
        started.append(
            send(unit, row.at[block_rows(ctx, tokens)], sems_x, d - 1, mates[d - 1])
        )
    own = [
        pltpu.make_async_copy(weights[a], outs[a].at[block_rows(shard, rows)], local.at[a])
        for a in range(count)
    ]
    own.append(pltpu.make_async_copy(unit, row.at[block_rows(ctx, tokens)], local.at[count]))
    own.append(pltpu.make_async_copy(gain, gains.at[shard], local.at[count + 1]))
    for item in own:
        item.start()
    across = {}
    other = lax.rem(far, WAYS)

    def relay(d):
        source = lax.rem(shard - d + n_shard, n_shard)
        for a in range(count):
            across[d, a].wait_recv()
            block = outs[a].at[block_rows(source, rows), columns(other, widths[a])]
            started.append(send(block, block, sems_c, (d - 1, a), (shard, near, tp)))

    for d in range(1, n_shard):
        source = lax.rem(shard - d + n_shard, n_shard)
        for a in range(count):
            first[d, a].wait_recv()
            block = outs[a].at[block_rows(source, rows), columns(member, widths[a])]
            across[d, a] = send(block, block, sems_f, (d - 1, a), (shard, far, tp))
            started.append(send(block, block, sems_n, (d - 1, a), (shard, near, tp)))
        if d > 1:
            relay(d - 1)
    relay(n_shard - 1)
    for item in started:
        item.wait()
    for item in list(first.values()) + list(across.values()):
        item.wait_send()
    for item in own:
        item.wait()


def gather_all(n_shard, n_ctx, weights, unit, gain):
    count = len(weights)
    grid = pltpu.SemaphoreType.DMA((n_shard - 1, count))
    return pl.pallas_call(
        functools.partial(gather_kernel, n_shard, n_ctx, count),
        out_shape=[
            jax.ShapeDtypeStruct((item.shape[0] * n_shard, item.shape[1]), item.dtype)
            for item in weights
        ]
        + [
            jax.ShapeDtypeStruct((unit.shape[0] * n_ctx, unit.shape[1]), unit.dtype),
            jax.ShapeDtypeStruct((n_shard,) + gain.shape, gain.dtype),
        ],
        in_specs=[vmem()] * (count + 2),
        out_specs=[vmem()] * (count + 2),
        scratch_shapes=[grid] * 8
        + [pltpu.SemaphoreType.DMA((n_ctx - 1,))] * 2
        + [pltpu.SemaphoreType.DMA((n_shard - 1,))] * 2
        + [pltpu.SemaphoreType.DMA((count + 2,))],
        compiler_params=params(0),
        name="gather_all",
    )(*weights, unit, gain)


def tp_kernel(n_tp, part, out, inbox, send_sem, recv_sem):
    shard, ctx, tp = (lax.axis_index("shard"), lax.axis_index("ctx"), lax.axis_index("tp"))
    peers = [(shard, ctx, lax.rem(tp + d, n_tp)) for d in range(1, n_tp)]
    greet(peers)
    copies = [
        send(part, inbox.at[d - 1], (send_sem, recv_sem), d - 1, peers[d - 1])
        for d in range(1, n_tp)
    ]
    total = part[...].astype(jnp.float32)
    for d in range(1, n_tp):
        copies[d - 1].wait_recv()
        total = total + inbox[d - 1].astype(jnp.float32)
    out[...] = total
    for copy in copies:
        copy.wait_send()


def tp_sum(value, n_tp, number):
    part = value.astype(jnp.bfloat16)
    return pl.pallas_call(
        functools.partial(tp_kernel, n_tp),
        out_shape=jax.ShapeDtypeStruct(part.shape, jnp.float32),
        in_specs=[vmem()],
        out_specs=vmem(),
        scratch_shapes=[
            pltpu.VMEM((n_tp - 1,) + part.shape, jnp.bfloat16),
            pltpu.SemaphoreType.DMA((n_tp - 1,)),
            pltpu.SemaphoreType.DMA((n_tp - 1,)),
        ],
        compiler_params=params(number),
        name=f"tp_sum{number}",
    )(part)


def tail_kernel(n_shard, n_ctx, n_tp, early, *refs):
    ready = refs[:early]
    (terms, dqp, qw, kvw, xn1_t, cosine, sine, kunit, rk, g_k, unit1, r1, g_ai, dh1, gain) = refs[
        early : early + 15
    ]
    refs = refs[early + 15 :]
    count = early + 2
    kv_at = count - 1
    outs, gain_out, input_grad = (refs[: count + 1], refs[count + 1], refs[count + 2])
    (late_q, late_kv, dkv_in, part, part_in) = refs[count + 3 : count + 8]
    (half, away, inbox, mine, arrived, done, kv_in, groups_in, shared) = refs[
        count + 8 : count + 17
    ]
    (g_own, g_near, g_far, g_mid, g_shard, g_group, g_tp) = refs[count + 17 : count + 24]
    sems = refs[count + 24 :]
    pair = [(sems[2 * k], sems[2 * k + 1]) for k in range(len(sems) // 2)]
    (
        s_core,
        s_far,
        s_shard,
        s_group,
        s_kv,
        s_share,
        s_gain,
        s_gz,
        s_gg,
        s_gt,
        s_dkv,
        s_part,
    ) = pair
    grads = list(ready) + [late_q, late_kv]
    shard, ctx, tp, near, far = place(n_ctx)
    n_groups = n_ctx // WAYS
    group = lax.div(ctx, WAYS)
    member, other = (lax.rem(ctx, WAYS), lax.rem(far, WAYS))
    beside = lax.rem(near, WAYS)
    opposite = beside + other - member
    rows = outs[0].shape[0]
    tokens = dqp.shape[0]
    widths = [item.shape[1] // WAYS for item in grads]
    starts = [sum(widths[:a]) for a in range(count)]
    batches = (list(range(early)), [early, early + 1])
    spans = (
        pl.ds(0, starts[early]),
        pl.ds(starts[early], widths[early] + widths[early + 1]),
    )
    near_id, far_id = ((shard, near, tp), (shard, far, tp))
    z_ids = [(lax.rem(shard + d, n_shard), ctx, tp) for d in range(1, n_shard)]
    c_ids = [(shard, lax.rem(ctx + d, n_ctx), tp) for d in range(1, n_ctx)]
    g_ids = [(shard, lax.rem(ctx + WAYS * d, n_ctx), tp) for d in range(1, n_groups)]
    t_ids = [(shard, ctx, lax.rem(tp + d, n_tp)) for d in range(1, n_tp)]
    greet(z_ids + c_ids + t_ids)

    ends = []
    core = {}
    over = {}
    along = {}
    order = list(range(1, n_shard)) + [0]
    targets = [lax.rem(shard + d, n_shard) for d in range(n_shard)]

    def start_core(batch):
        for slot, quarter in ((1, opposite), (0, beside)):
            for d in order:
                where = block_rows(targets[d], rows)
                for a in batches[batch]:
                    core[slot, a, d] = send(
                        grads[a].at[where, columns(quarter, widths[a])],
                        half.at[slot, where, pl.ds(starts[a], widths[a])],
                        s_core,
                        (slot, a, d),
                        near_id,
                    )

    def start_over(batch):
        for d in order:
            where = block_rows(targets[d], rows)
            for a in batches[batch]:
                core[1, a, d].wait_recv()
                cols = pl.ds(starts[a], widths[a])
                total = half[1, where, cols].astype(jnp.float32) + grads[a][
                    where, columns(other, widths[a])
                ].astype(jnp.float32)
                away[where, cols] = total.astype(jnp.bfloat16)
            over[batch, d] = send(
                away.at[where, spans[batch]],
                inbox.at[where, spans[batch]],
                s_far,
                (batch, d),
                far_id,
            )

    def start_along(batch):
        for d in order:
            where = block_rows(targets[d], rows)
            over[batch, d].wait_recv()
            for a in batches[batch]:
                core[0, a, d].wait_recv()
                cols = pl.ds(starts[a], widths[a])
                total = (
                    half[0, where, cols].astype(jnp.float32)
                    + grads[a][where, columns(member, widths[a])].astype(jnp.float32)
                    + inbox[where, cols].astype(jnp.float32)
                )
                mine[where, cols] = total.astype(jnp.bfloat16)
            if d:
                along[batch, d] = send(
                    mine.at[where, spans[batch]],
                    arrived.at[d - 1, :, spans[batch]],
                    s_shard,
                    (batch, d - 1),
                    z_ids[d - 1],
                )

    def finish(batch):
        span = spans[batch]
        total = mine[block_rows(shard, rows), span].astype(jnp.float32)
        for d in range(1, n_shard):
            along[batch, d].wait_recv()
            total = total + arrived[d - 1, :, span].astype(jnp.float32)
        if n_groups > 1:
            groups_in[group, :, span] = total.astype(jnp.bfloat16)
            piece = groups_in.at[group, :, span]
            moved = [
                send(piece, piece, s_group, (batch, d - 1), g_ids[d - 1])
                for d in range(1, n_groups)
            ]
            for item in moved:
                item.wait_recv()
            ends.extend(moved)
            total = groups_in[0, :, span].astype(jnp.float32)
            for g in range(1, n_groups):
                total = total + groups_in[g, :, span].astype(jnp.float32)
        return total.astype(jnp.bfloat16)

    def start_share(batch):
        piece = shared.at[member, :, spans[batch]]
        return (
            send(piece, piece, s_share, (batch, 0), far_id),
            send(piece, piece, s_share, (batch, 1), near_id),
        )

    def relay_share(batch, first):
        first[0].wait_recv()
        piece = shared.at[other, :, spans[batch]]
        return send(piece, piece, s_share, (batch, 2), near_id)

    scatter = [
        send(
            terms.at[block_rows(c_ids[d - 1][1], tokens)],
            dkv_in.at[d - 1],
            s_dkv,
            d - 1,
            c_ids[d - 1],
        )
        for d in range(1, n_ctx)
    ]
    start_core(0)
    late_q[...] = dot_plain(xn1_t[...], dqp[...]).astype(jnp.bfloat16)
    start_over(0)
    dxn1 = dot_last(dqp[...], qw[...])
    dkv = terms[block_rows(ctx, tokens), :].astype(jnp.float32)
    for d in range(1, n_ctx):
        scatter[d - 1].wait_recv()
        dkv = dkv + dkv_in[d - 1].astype(jnp.float32)
    dkn = unrotate(dkv[:, :HD], cosine[...], sine[...])
    dg_k = jnp.sum(dkn * kunit[...], axis=0, keepdims=True)
    dkp = norm_back(dkn * g_k[...], kunit[...], rk[...]).astype(jnp.bfloat16)
    dkvp = jnp.concatenate([dkp, dkv[:, HD:].astype(jnp.bfloat16)], axis=1)
    part[...] = (dxn1 + dot_last(dkvp, kvw[...])).astype(jnp.bfloat16)
    parts = [
        send(part, part_in.at[d - 1], s_part, d - 1, t_ids[d - 1]) for d in range(1, n_tp)
    ]
    late_kv[...] = dot_plain(xn1_t[...], dkvp).astype(jnp.bfloat16)
    start_core(1)
    dxn1 = part[...].astype(jnp.float32)
    for d in range(1, n_tp):
        parts[d - 1].wait_recv()
        dxn1 = dxn1 + part_in[d - 1].astype(jnp.float32)
    dg_ai = jnp.sum(dxn1 * unit1[...], axis=0, keepdims=True) * (1.0 / n_tp)
    input_grad[...] = dh1[...] + norm_back(dxn1 * g_ai[...], unit1[...], r1[...])
    g_own[...] = gain[...]
    at = 0
    for line in (dg_ai, dg_k):
        for k in range(line.shape[1] // LANES):
            g_own[pl.ds(at, 1), :] = line[:, k * LANES : (k + 1) * LANES]
            at = at + 1
    gain_near = send(g_own, g_near, s_gain, 0, near_id)
    start_over(1)
    gain_near.wait_recv()
    g_mid[0] = g_own[...] + g_near[...]
    gain_far = send(g_mid.at[0], g_far, s_gain, 1, far_id)

    start_along(0)
    gain_far.wait_recv()
    g_shard[shard] = g_mid[0] + g_far[...]
    gz = [
        send(g_shard.at[shard], g_shard.at[shard], s_gz, d - 1, z_ids[d - 1])
        for d in range(1, n_shard)
    ]
    start_along(1)
    shared[member, :, spans[0]] = finish(0)
    share0 = start_share(0)

    for item in gz:
        item.wait_recv()
    total = g_shard[0]
    for k in range(1, n_shard):
        total = total + g_shard[k]
    g_group[group] = total
    gg = [
        send(g_group.at[group], g_group.at[group], s_gg, d - 1, g_ids[d - 1])
        for d in range(1, n_groups)
    ]
    for item in gg:
        item.wait_recv()
    total = g_group[0]
    for k in range(1, n_groups):
        total = total + g_group[k]
    g_tp[tp] = total
    gt = [
        send(g_tp.at[tp], g_tp.at[tp], s_gt, d - 1, t_ids[d - 1]) for d in range(1, n_tp)
    ]

    done[...] = finish(1)
    kv_cols = pl.ds(widths[early], widths[kv_at])
    kvs = [
        send(done.at[:, kv_cols], kv_in.at[d - 1], s_kv, d - 1, t_ids[d - 1])
        for d in range(1, n_tp)
    ]
    relay0 = relay_share(0, share0)
    shared[member, :, pl.ds(starts[early], widths[early])] = done[:, pl.ds(0, widths[early])]
    total = done[:, kv_cols].astype(jnp.float32)
    for d in range(1, n_tp):
        kvs[d - 1].wait_recv()
        total = total + kv_in[d - 1].astype(jnp.float32)
    shared[member, :, pl.ds(starts[kv_at], widths[kv_at])] = total.astype(jnp.bfloat16)
    share1 = start_share(1)
    for item in gt:
        item.wait_recv()
    total = g_tp[0]
    for k in range(1, n_tp):
        total = total + g_tp[k]
    gain_out[...] = total

    def write(batch):
        for q in range(WAYS):
            for a in batches[batch]:
                value = shared[q, :, pl.ds(starts[a], widths[a])]
                if a == kv_at:
                    out = outs[a] if q < WAYS // 2 else outs[count]
                    out[:, pl.ds((q % (WAYS // 2)) * widths[a], widths[a])] = value
                else:
                    outs[a][:, pl.ds(q * widths[a], widths[a])] = value

    share0[1].wait_recv()
    relay0.wait_recv()
    write(0)
    relay1 = relay_share(1, share1)
    share1[1].wait_recv()
    relay1.wait_recv()
    write(1)
    ends.extend(scatter + parts + list(core.values()) + list(over.values()))
    ends.extend(list(along.values()) + kvs + gz + gg + gt + [gain_near, gain_far])
    ends.extend(list(share0) + list(share1) + [relay0, relay1])
    for item in ends:
        item.wait_send()


def run_tail(n_shard, n_ctx, n_tp, ready, terms, dqp, qw, kvw, xn1_t, small, dh1, gain):
    deep = qw.shape[0]
    tokens = dqp.shape[0]
    rows = deep // n_shard
    n_groups = n_ctx // WAYS
    early = len(ready)
    count = early + 2
    late = (qw.shape[1], kvw.shape[1])
    wide = sum([item.shape[1] // WAYS for item in ready]) + sum(late) // WAYS
    out_widths = [item.shape[1] for item in ready] + [late[0], late[1] // 2, late[1] // 2]
    low, full = (jnp.bfloat16, jnp.float32)
    operands = (*ready, terms, dqp, qw, kvw, xn1_t, *small, dh1, gain)

    def dma(*shape):
        return [pltpu.SemaphoreType.DMA(shape)] * 2

    return pl.pallas_call(
        functools.partial(tail_kernel, n_shard, n_ctx, n_tp, early),
        out_shape=[jax.ShapeDtypeStruct((rows, item), low) for item in out_widths]
        + [jax.ShapeDtypeStruct(gain.shape, full), jax.ShapeDtypeStruct(dh1.shape, full)],
        in_specs=[vmem()] * len(operands),
        out_specs=[vmem()] * (count + 3),
        scratch_shapes=[
            pltpu.VMEM((deep, late[0]), low),
            pltpu.VMEM((deep, late[1]), low),
            pltpu.VMEM((n_ctx - 1, tokens, terms.shape[1]), low),
            pltpu.VMEM((tokens, deep), low),
            pltpu.VMEM((n_tp - 1, tokens, deep), low),
            pltpu.VMEM((2, deep, wide), low),
            pltpu.VMEM((deep, wide), low),
            pltpu.VMEM((deep, wide), low),
            pltpu.VMEM((deep, wide), low),
            pltpu.VMEM((n_shard - 1, rows, wide), low),
            pltpu.VMEM((rows, sum(late) // WAYS), low),
            pltpu.VMEM((n_tp - 1, rows, late[1] // WAYS), low),
            pltpu.VMEM((n_groups, rows, wide), low),
            pltpu.VMEM((WAYS, rows, wide), low),
            pltpu.VMEM(gain.shape, full),
            pltpu.VMEM(gain.shape, full),
            pltpu.VMEM(gain.shape, full),
            pltpu.VMEM((1,) + gain.shape, full),
            pltpu.VMEM((n_shard,) + gain.shape, full),
            pltpu.VMEM((n_groups,) + gain.shape, full),
            pltpu.VMEM((n_tp,) + gain.shape, full),
        ]
        + dma(2, count, n_shard)
        + dma(2, n_shard)
        + dma(2, n_shard - 1)
        + dma(2, max(n_groups - 1, 1))
        + dma(n_tp - 1)
        + dma(2, 3)
        + dma(2)
        + dma(n_shard - 1)
        + dma(max(n_groups - 1, 1))
        + dma(n_tp - 1)
        + dma(n_ctx - 1)
        + dma(n_tp - 1),
        compiler_params=params(6),
        name="tail",
    )(*operands)


def pack_lanes(items):
    flat = jnp.concatenate([item.astype(jnp.float32) for item in items])
    unit = 8 * LANES
    short = -flat.shape[0] % unit
    return jnp.pad(flat, (0, short)).reshape(-1, LANES)


def per_device(
    block_input,
    out_cotangent,
    seq_lengths,
    q_weight,
    k_weight,
    v_weight,
    o_weight,
    gate_weight,
    up_weight,
    down_weight,
    attn_in_gain,
    attn_out_gain,
    ffn_in_gain,
    ffn_out_gain,
    query_gain,
    key_gain,
):
    tokens = block_input.shape[0]
    width = block_input.shape[1]
    n_ctx = lax.axis_size("ctx")
    n_tp = lax.axis_size("tp")
    row_len = tokens * n_ctx
    n_shard = lax.axis_size("shard")
    my_start = lax.axis_index("ctx") * tokens
    scaling = HD ** (-0.5)
    segment, position = layout(seq_lengths[0], row_len)
    key_index = jnp.arange(row_len)
    query_index = my_start + jnp.arange(tokens)
    query_seg = lax.dynamic_slice_in_dim(segment, my_start, tokens)
    allowed = (query_seg[:, None] == segment[None, :]) & (
        key_index[None, :] <= query_index[:, None]
    )
    row_cosine, row_sine = rope_tables(position)
    cosine = lax.dynamic_slice_in_dim(row_cosine, my_start, tokens)
    sine = lax.dynamic_slice_in_dim(row_sine, my_start, tokens)
    unit1, r1 = norm_parts(block_input)
    gains = (attn_in_gain, attn_out_gain, ffn_in_gain, ffn_out_gain, query_gain, key_gain)
    qw, kvw, ow, gw, uw, dw, unit_row, packed = gather_all(
        n_shard,
        n_ctx,
        (
            q_weight,
            jnp.concatenate([k_weight, v_weight], axis=1),
            o_weight,
            gate_weight,
            up_weight,
            down_weight,
        ),
        unit1.astype(jnp.bfloat16),
        pack_lanes(gains),
    )
    packed = packed.reshape(n_shard, -1)
    split = []
    at = 0
    for item in gains:
        split.append(packed[:, at : at + item.shape[0]].reshape(-1))
        at = at + item.shape[0]
    g_ai, g_ao, g_fi, g_fo, g_q, g_k = split
    local_heads = qw.shape[1] // HD
    xn1 = (unit1 * g_ai).astype(jnp.bfloat16)
    qp = dot_plain(xn1, qw).reshape(tokens, local_heads, HD)
    qunit, rq = norm_parts(qp)
    queries = rotate(qunit * g_q, cosine[:, None, :], sine[:, None, :]).astype(jnp.bfloat16)
    xn1_row = (unit_row.astype(jnp.float32) * g_ai).astype(jnp.bfloat16)
    kvp = dot_plain(xn1_row, kvw)
    row_kunit, row_rk = norm_parts(kvp[:, :HD])
    row_keys = rotate(row_kunit * g_k, row_cosine, row_sine).astype(jnp.bfloat16)
    row_values = kvp[:, HD:].astype(jnp.bfloat16)
    kunit = lax.dynamic_slice_in_dim(row_kunit, my_start, tokens)
    rk = lax.dynamic_slice_in_dim(row_rk, my_start, tokens)
    head_outs = []
    lses = []
    for head in range(local_heads):
        logits = masked_scores(queries[:, head, :], row_keys, allowed, scaling)
        peak = jnp.max(logits, axis=1, keepdims=True)
        lse = peak + jnp.log(jnp.sum(jnp.exp(logits - peak), axis=1, keepdims=True))
        weights = jnp.exp(logits - lse).astype(jnp.bfloat16)
        head_outs.append(dot_plain(weights, row_values))
        lses.append(lse)
    attended = jnp.concatenate(head_outs, axis=1).astype(jnp.bfloat16)
    proj = tp_sum(dot_last(attended, ow), n_tp, 1)
    aunit, ra = norm_parts(proj)
    h1 = block_input + aunit * g_ao
    unit2, r2 = norm_parts(h1)
    xn2 = (unit2 * g_fi).astype(jnp.bfloat16)
    gate = dot_plain(xn2, gw)
    up = dot_plain(xn2, uw)
    act, gelu_back = jax.vjp(gelu_tanh, gate)
    hidden = (act * up).astype(jnp.bfloat16)
    ffn = tp_sum(dot_last(hidden, dw), n_tp, 2)
    funit, rf = norm_parts(ffn)
    block_output = h1 + funit * g_fo
    back_keys, back_values = (row_keys, row_values)
    dg_fo = jnp.sum(out_cotangent * funit, axis=0)
    dffn = norm_back(out_cotangent * g_fo, funit, rf).astype(jnp.bfloat16)
    dhid = dot_plain(dffn, dw)
    d_down = dot_first(dffn, hidden)
    dup = (dhid * act).astype(jnp.bfloat16)
    dgate = gelu_back(dhid * up)[0].astype(jnp.bfloat16)
    d_gate_w = dot_first(xn2, dgate)
    d_up_w = dot_first(xn2, dup)
    dxn2 = tp_sum(dot_last(dgate, gw) + dot_last(dup, uw), n_tp, 3)
    dg_fi = jnp.sum(dxn2 * unit2, axis=0)
    dh1 = out_cotangent + norm_back(dxn2 * g_fi, unit2, r2)
    dg_ao = jnp.sum(dh1 * aunit, axis=0)
    dproj = norm_back(dh1 * g_ao, aunit, ra).astype(jnp.bfloat16)
    d_o_w = dot_first(dproj, attended)
    dattended = dot_plain(dproj, ow).astype(jnp.bfloat16)
    win_keys, win_values, win_allowed = (back_keys, back_values, allowed)
    key_terms = jnp.zeros((row_len, HD), jnp.float32)
    value_terms = jnp.zeros((row_len, HD), jnp.float32)
    dq_parts = []
    for head in range(local_heads):
        query_head = queries[:, head, :]
        out_head = attended[:, head * HD : (head + 1) * HD]
        dout_head = dattended[:, head * HD : (head + 1) * HD]
        logits = masked_scores(query_head, win_keys, win_allowed, scaling)
        weights = jnp.exp(logits - lses[head])
        weights_low = weights.astype(jnp.bfloat16)
        delta = jnp.sum(
            dout_head.astype(jnp.float32) * out_head.astype(jnp.float32), axis=1, keepdims=True
        )
        dprob = dot_last(dout_head, win_values)
        dscore = (weights * (dprob - delta) * scaling).astype(jnp.bfloat16)
        dq_parts.append(dot_plain(dscore, win_keys))
        key_terms = key_terms + dot_first(dscore, query_head)
        value_terms = value_terms + dot_first(weights_low, dout_head)
    dq = jnp.stack(dq_parts, axis=1)
    dqn = unrotate(dq, cosine[:, None, :], sine[:, None, :])
    dg_q = jnp.sum(dqn * qunit, axis=(0, 1))
    dqp = norm_back(dqn * g_q, qunit, rq).reshape(tokens, local_heads * HD).astype(jnp.bfloat16)
    terms = jnp.concatenate([key_terms, value_terms], axis=1).astype(jnp.bfloat16)
    ready = [item.astype(jnp.bfloat16) for item in (d_o_w, d_gate_w, d_up_w, d_down)]
    share = 1.0 / n_tp
    late = (jnp.zeros((width,), jnp.float32), jnp.zeros((HD,), jnp.float32))
    sums = (*late, dg_ao * share, dg_fi * share, dg_fo * share, dg_q)
    outs = run_tail(
        n_shard,
        n_ctx,
        n_tp,
        ready,
        terms,
        dqp,
        qw,
        kvw,
        xn1.T,
        (cosine, sine, kunit, rk, g_k[None, :], unit1, r1, g_ai[None, :]),
        dh1,
        pack_lanes(sums),
    )
    o_out, gate_out, up_out, down_out, q_out, k_out, v_out = [
        item.astype(jnp.float32) for item in outs[:7]
    ]
    gain_sums, input_grad = outs[7:]
    flat = gain_sums.reshape(-1)
    gain_outs = []
    at = 0
    for term in sums:
        own = term.shape[0] // n_shard
        gain_outs.append(
            lax.dynamic_slice_in_dim(flat, at + lax.axis_index("shard") * own, own)
        )
        at = at + term.shape[0]
    dg_ai, dg_k, dg_ao, dg_fi, dg_fo, dg_q = gain_outs
    return (
        block_output,
        input_grad,
        q_out,
        k_out,
        v_out,
        o_out,
        gate_out,
        up_out,
        down_out,
        dg_ai,
        dg_ao,
        dg_fi,
        dg_fo,
        dg_q,
        dg_k,
    )


def solution(mesh):
    placed = (
        P(("shard", "ctx"), None),
        P(("shard", "ctx"), None),
        P("shard", None),
        P("shard", "tp"),
        P("shard", None),
        P("shard", None),
        P("shard", "tp"),
        P("shard", "tp"),
        P("shard", "tp"),
        P("shard", "tp"),
        P("shard"),
        P("shard"),
        P("shard"),
        P("shard"),
        P("shard"),
        P("shard"),
    )
    return jax.shard_map(
        per_device,
        mesh=mesh,
        in_specs=placed,
        out_specs=(
            P(("shard", "ctx"), None),
            P(("shard", "ctx"), None),
            P("shard", "tp"),
            P("shard", None),
            P("shard", None),
            P("shard", "tp"),
            P("shard", "tp"),
            P("shard", "tp"),
            P("shard", "tp"),
            P("shard"),
            P("shard"),
            P("shard"),
            P("shard"),
            P("shard"),
            P("shard"),
        ),
        check_vma=False,
    )
```
